128 devices in a mesh: trace: 8 (over y, core), gx: 4 (over z), gy: 4 (over x).
Axes of the slice: x: 4, y: 4, z: 4, core: 2. Of those that a mesh axis runs over, the one named last changes fastest.
Arguments:
- traces: bfloat16 [32768, 4, 256], P(('trace', 'gx', 'gy')), may hold values from -4 to 4
- coupling: bfloat16 [32768, 4], P(('trace', 'gx', 'gy')), may hold values from 0.099609375 to 1.8984375
- tap_shift: int32 [32768], P(('trace', 'gx', 'gy')), may hold values from 0 to 63
- node_tile: int32 [32768, 1], P(('trace', 'gx', 'gy')), may hold values from 0 to 127; in each aligned block of 256 rows (0 to 255, 256 to 511, ...) at most 4 rows name the same one
- node_cell: int32 [32768], P(('trace', 'gx', 'gy')), may hold values from 0 to 524287
- field_prev: float32 [64, 1024, 1024], P('trace', 'gx', 'gy'), may hold values from -0.3125 to 0.3125
- field_now: float32 [64, 1024, 1024], P('trace', 'gx', 'gy'), may hold values from -0.3125 to 0.3125
- speed_sq: float32 [64, 1024, 1024], P('trace', 'gx', 'gy'), may hold values from 0.3 to 1
Outputs:
- out_prev: float32 [64, 1024, 1024], P('trace', 'gx', 'gy')
- out_now: float32 [64, 1024, 1024], P('trace', 'gx', 'gy')
The draws below stay inside these ranges and needn't reach their ends.
Inputs may be any that keep to these rules, and one draw needn't show every extreme that they name: `node_tile`: among the nodes of one device at most 4 lie in one tile, and some device has exactly 4 in some tile.
All inputs are finite; a program needn't handle non-finite values.
Results may differ from the reference program's by a relative error of at most 0.0003.
Values may be sent and summed in bfloat16 or wider, within the bound.
A program may use at most 128 MiB of HBM per device.

```python
import math
import jax
import jax.numpy as jnp
import numpy as np
from jax import lax

CZ = 8
CX = 256
CY = 256
NODE_DEV = 256
NT = 256
STEPS = 4
COMP = 4
CAP = 4
RATE = 64
NODES = 32768
NZ = 64
NX = 1024
NY = 1024
N_GX = 4
N_GY = 4
DEVICES = 128


def touch_ends(entries, key, smallest, top_value):
    longest = entries.shape.index(max(entries.shape))
    spots = []
    for shift in (0, 1):
        where = [jax.random.randint(jax.random.fold_in(key, axis), (), 0, length) for axis, length in enumerate(entries.shape)]
        where[longest] = (where[longest] + shift) % entries.shape[longest]
        spots.append(tuple(where))
    return entries.at[spots[0]].set(smallest).at[spots[1]].set(top_value)


def steps_of(key, extent, cuts, least, top_value):
    gain, own = 1.0, jax.random.fold_in(key, 6)
    for position, shards_of in cuts:
        draws = jnp.exp(jax.random.uniform(jax.random.fold_in(own, position), (shards_of,), jnp.float32, least / len(cuts), top_value / len(cuts)))
        gain = gain * jnp.repeat(draws, extent[position] // shards_of).reshape([-1 if axis == position else 1 for axis in range(len(extent))])
    return gain


def shared_out(stream_key, own, number, rows, count, top, reach, lean):
    sequence = jax.random.permutation(stream_key, count)
    crowded, common = load_shares(count, rows * top, reach, lean, True), load_shares(count, rows * top, reach, lean, False)
    places = jnp.arange(count)

    def named(tallies, rotation):
        used = int((tallies > 0).sum())
        fixed = max(1, used // 4)
        moved = fixed + (places - fixed + rotation * (used - fixed)) % max(1, count - fixed)
        return jnp.zeros((count,), jnp.int32).at[sequence[jnp.where(places < fixed, places, moved)]].set(jnp.asarray(tallies, jnp.int32))

    tallies = jnp.where(number % 4 == 0, named(crowded, number // 4), named(common, number - number // 4 - 1))
    mixed = jax.random.permutation(jax.random.fold_in(own, 3), count)
    donor, receiver = mixed[0:count // 2 * 2:2], mixed[1:count // 2 * 2:2]
    margin = jnp.minimum(tallies[donor] - 1, reach - tallies[receiver]) // 2
    margin = jnp.where((donor == sequence[0]) | (receiver == sequence[0]) | (tallies[receiver] == 0), 0, jnp.maximum(margin, 0))
    moved = jax.random.randint(jax.random.fold_in(own, 4), (count // 2,), 0, 1 << 20) % (margin + 1)
    tallies = tallies.at[donor].add(-moved).at[receiver].add(moved)
    items = jnp.searchsorted(jnp.cumsum(tallies), jnp.arange(rows * top), side="right").astype(jnp.int32)
    listing = items.reshape(top, rows).T
    listing = listing[jax.random.permutation(jax.random.fold_in(own, 1), rows)]
    rotation = jax.random.randint(jax.random.fold_in(own, 2), (rows, 1), 0, top)
    return jnp.take_along_axis(listing, (jnp.arange(top)[None, :] + rotation) % top, axis=1)


def load_shares(count, total, reach, skew, full):
    weights = [(1 << 20) // math.isqrt(rank ** skew) + 1 for rank in range(1, count + 1)]
    largest = reach if full else min(reach, max(-(-total // count), total * weights[0] // sum(weights)))
    least = 1 if total - largest >= count - 1 else 0
    holding, rest = [largest] + [least] * (count - 1), total - largest - least * (count - 1)
    while rest > 0:
        free = [i for i in range(1, count) if holding[i] < largest] or [i for i in range(1, count) if holding[i] < reach]
        whole, left = sum([weights[i] for i in free]), rest
        for i in free:
            addition = min(reach - holding[i], max(1, left * weights[i] // whole), rest)
            holding[i] = holding[i] + addition
            rest = rest - addition
    return np.array(holding)


def scatter_about(key, extent, spread, most, cuts=(), kind=jnp.bfloat16):
    values = spread * jax.random.normal(key, extent, jnp.float32)
    if cuts:
        values = values * steps_of(key, extent, cuts, -0.22, 0.18)
    return jnp.clip(values, -most, most).astype(kind)


def setup_inputs(seed: int = 0) -> dict:
    arg_keys = jax.random.split(jax.random.key(seed), 9)
    traces = scatter_about(arg_keys[0], (NODES, COMP, NT), 0.25, 4.0, ((0, 128),))
    coupling = jnp.clip(1.0 + 0.18 * jax.random.normal(arg_keys[1], (NODES, COMP), jnp.float32), 0.099609375, 1.8984375).astype(jnp.bfloat16)
    tap_shift = touch_ends(jax.random.randint(arg_keys[2], (NODES,), 0, RATE), jax.random.fold_in(arg_keys[2], 1), 0, RATE - 1).astype(jnp.int32)
    node_tile_keys = jax.random.split(jax.random.fold_in(arg_keys[3], 1), NODES // NODE_DEV)
    node_tile_turns = jax.random.permutation(jax.random.fold_in(arg_keys[3], 3), NODES // NODE_DEV)
    node_tile = jax.vmap(lambda own, number: shared_out(jax.random.fold_in(arg_keys[3], 2), own, number, NODE_DEV, DEVICES, 1, CAP, 2))(node_tile_keys, node_tile_turns).reshape((NODES, 1))
    node_cell = touch_ends(jax.random.randint(arg_keys[4], (NODES,), 0, CZ * CX * CY), jax.random.fold_in(arg_keys[4], 1), 0, (CZ * CX * CY) - 1).astype(jnp.int32)
    field_prev = scatter_about(arg_keys[5], (NZ, NX, NY), ((CZ * CX * CY // NODE_DEV) ** -0.5), 0.3125, ((0, 8), (1, 4), (2, 4)), jnp.float32)
    field_now = scatter_about(arg_keys[6], (NZ, NX, NY), ((CZ * CX * CY // NODE_DEV) ** -0.5), 0.3125, ((0, 8), (1, 4), (2, 4)), jnp.float32)
    speed_sq = jnp.clip(0.3 + 0.7 * jax.random.uniform(arg_keys[7], (NZ, NX, NY), jnp.float32) ** steps_of(arg_keys[7], (NZ, NX, NY), ((0, 8), (1, 4), (2, 4)), -0.2, 0.2), 0.3, 1.0)
    return {"traces": traces, "coupling": coupling, "tap_shift": tap_shift, "node_tile": node_tile, "node_cell": node_cell, "field_prev": field_prev, "field_now": field_now, "speed_sq": speed_sq}


def make_kernel(shift_values):
    samples = jnp.arange(NT).astype(jnp.float32)
    step_numbers = jnp.arange(STEPS).astype(jnp.float32)
    centre = (NT - RATE // 2) - RATE * step_numbers[None, :] - shift_values.astype(jnp.float32)[:, None]
    offset = samples[None, None, :] - centre[:, :, None]
    window = 0.5 * (1.0 + jnp.cos(math.pi * offset / (2.0 * RATE)))
    inside = jnp.abs(offset) < 2.0 * RATE
    return jnp.where(inside, jnp.sinc(offset / RATE) * window, jnp.zeros_like(offset))


def resample(traces, coupling, shift_values):
    kernel = make_kernel(shift_values)
    combined = jnp.sum(traces.astype(jnp.float32) * coupling.astype(jnp.float32)[:, :, None], axis=1)
    return jnp.einsum("nt,nst->ns", combined, kernel, precision=lax.Precision.HIGHEST)


def laplace(field):
    padded = jnp.pad(field, 1)
    beside = padded[2:, 1:-1, 1:-1] + padded[:-2, 1:-1, 1:-1]
    beside = beside + padded[1:-1, 2:, 1:-1] + padded[1:-1, :-2, 1:-1]
    beside = beside + padded[1:-1, 1:-1, 2:] + padded[1:-1, 1:-1, :-2]
    return beside - 6.0 * field


def reference(traces, coupling, tap_shift, node_tile, node_cell, field_prev, field_now, speed_sq):
    amplitudes = resample(traces, coupling, tap_shift)
    tile_ids = node_tile[:, 0]
    slab_index = tile_ids // (N_GX * N_GY)
    first_tile = (tile_ids // N_GY) % N_GX
    second_tile = tile_ids % N_GY
    depth_cell = node_cell // (CX * CY)
    first_cell = (node_cell // CY) % CX
    second_cell = node_cell % CY
    global_index = ((slab_index * CZ + depth_cell) * NX + first_tile * CX + first_cell) * NY + second_tile * CY + second_cell
    global_index = global_index.astype(jnp.int32)
    for step_index in range(STEPS):
        source = jnp.zeros((NZ * NX * NY,), jnp.float32).at[global_index].add(amplitudes[:, step_index]).reshape(NZ, NX, NY)
        nextfield = 2.0 * field_now - field_prev + 0.25 * speed_sq * (laplace(field_now) + source)
        field_prev = field_now
        field_now = nextfield
    return field_prev, field_now
```

```python
import functools
import math

import jax
import jax.numpy as jnp
import numpy as np
from jax import lax
from jax.experimental import pallas as pl
from jax.experimental.pallas import tpu as pltpu
from jax.sharding import PartitionSpec as P

NT = 256
STEPS = 4
RATE = 64
CZ, CX, CY = 8, 256, 256
NT_AX, NGX, NGY = 8, 4, 4
CAP = 4
PAD = 8
ROWS = 32
MESH = pl.DeviceIdType.MESH
F32 = jnp.float32
BF16 = jnp.bfloat16


def window_table():
    u = (np.arange(NT)[None, :] + np.arange(NT)[:, None] - (NT - RATE // 2)).astype(np.float64)
    w = np.sinc(u / RATE) * 0.5 * (1.0 + np.cos(math.pi * u / (2.0 * RATE)))
    return np.where(np.abs(u) < 2.0 * RATE, w, 0.0).astype(np.float32)


def nt_dot(a, b, precision=None):
    return lax.dot_general(
        a, b, (((1,), (1,)), ((), ())), precision=precision, preferred_element_type=F32
    )


def kernel(
    comb_ref, win_ref, shift_ref, tile_ref, cell_ref, prev_hbm, now_hbm, speed_hbm,
    outp_hbm, outn_hbm,
    fa, fb, q, s_ref, gz, gx_buf, gy_buf, px, py, hy, rows_1h, v_hi, v_lo, t1, b1, b2, b3, b4,
    lsem, osem, zs, zr, xs, xr, ys, yr, a_s, a_r,
):
    t = lax.axis_index("trace")
    gx = lax.axis_index("gx")
    gy = lax.axis_index("gy")

    loads = [
        pltpu.make_async_copy(now_hbm, fa.at[:, pl.ds(PAD, CX), :], lsem.at[0]),
        pltpu.make_async_copy(prev_hbm, fb.at[:, pl.ds(PAD, CX), :], lsem.at[1]),
        pltpu.make_async_copy(speed_hbm, q, lsem.at[2]),
    ]
    for c in loads:
        c.start()

    sides = (("trace", t, NT_AX), ("gx", gx, NGX), ("gy", gy, NGY))
    for buf, (_, pos, count) in zip((gz, gx_buf, gy_buf), sides):
        for side in (0, 1):
            @pl.when(pos == (0 if side == 0 else count - 1))
            def _(buf=buf, side=side):
                for k in range(STEPS):
                    buf[k, side] = jnp.zeros(buf.shape[2:], F32)

    barrier = pltpu.get_barrier_semaphore()
    peers = []
    for axis, pos, count in sides:
        for d in range(1, count):
            peers.append((axis, lax.rem(pos + d, count)))
    for axis, j in peers:
        pl.semaphore_signal(barrier, inc=1, device_id={axis: j}, device_id_type=MESH)
    pl.semaphore_wait(barrier, len(peers))

    def halo(kind, k, d, src=None):
        axis, pos, count = sides[kind]
        ghost = (gz, gx_buf, gy_buf)[kind]
        ssem, rsem = ((zs, zr), (xs, xr), (ys, yr))[kind]
        if src is None:
            src = ghost.at[k, 1 - d]
        to = jnp.maximum(pos - 1, 0) if d == 0 else jnp.minimum(pos + 1, count - 1)
        return pltpu.make_async_remote_copy(
            src_ref=src,
            dst_ref=ghost.at[k, 1 - d],
            send_sem=ssem.at[k, d],
            recv_sem=rsem.at[k, 1 - d],
            device_id={axis: to},
            device_id_type=MESH,
        )

    def exists(kind, d):
        _, pos, count = sides[kind]
        return pos > 0 if d == 0 else pos < count - 1

    def send(kind, k, d, src):
        @pl.when(exists(kind, d))
        def _():
            halo(kind, k, d, src).start()

    def wait_ghost(kind, k):
        for side in (0, 1):
            @pl.when(exists(kind, side))
            def _(side=side):
                halo(kind, k, 1 - side).wait_recv()

    def wait_sent(kind, k):
        for d in (0, 1):
            @pl.when(exists(kind, d))
            def _(d=d):
                halo(kind, k, d).wait_send()

    send(0, 0, 0, now_hbm.at[0])
    send(0, 0, 1, now_hbm.at[CZ - 1])

    at = nt_dot(win_ref[...], comb_ref[...], lax.Precision.HIGHEST)
    shift = shift_ref[...]
    picked = lax.broadcasted_iota(jnp.int32, (RATE, NT), 0) == shift
    amps = [
        jnp.sum(jnp.where(picked, at[s * RATE:(s + 1) * RATE, :], 0.0), axis=0, keepdims=True)
        for s in range(STEPS)
    ]
    cell = cell_ref[...]
    cz = (cell // (CX * CY)).astype(F32)
    cx = ((cell // CY) % CX).astype(F32)
    cy = (cell % CY).astype(F32)
    hi = [a.astype(BF16).astype(F32) for a in amps]
    lo = [a - h for a, h in zip(amps, hi)]
    zero_row = jnp.zeros((1, NT), F32)
    vals = jnp.concatenate([cz, cx, cy] + hi + lo + [zero_row] * 5, axis=0).astype(BF16)
    tile = tile_ref[...]
    dest = (tile % NGY) * (NGX * NT_AX) + ((tile // NGY) % NGX) * NT_AX + tile // (NGX * NGY)
    n_dev = NT_AX * NGX * NGY
    onehot = lax.broadcasted_iota(jnp.int32, (n_dev, NT), 0) == dest
    onehot_f = jnp.where(onehot, 1.0, 0.0)
    before = jnp.where(
        lax.broadcasted_iota(jnp.int32, (NT, NT), 0) < lax.broadcasted_iota(jnp.int32, (NT, NT), 1),
        1.0, 0.0,
    ).astype(BF16)
    rank = jnp.dot(onehot_f.astype(BF16), before, preferred_element_type=F32)
    table = jnp.zeros((n_dev, 128), F32)
    for j in range(CAP):
        picks = jnp.where(rank == float(j), onehot_f, 0.0).astype(BF16)
        parts = []
        if j:
            parts.append(jnp.zeros((16 * j, NT), BF16))
        parts.append(vals)
        parts.append(jnp.zeros((128 - 16 * (j + 1), NT), BF16))
        table = table + nt_dot(picks, jnp.concatenate(parts, axis=0))
    t1[...] = table.reshape(NGY, NGX, NT_AX, 128)

    def exchange(phase, axis, pos, count, src_of, dst):
        def copy(d, to_or_from):
            return pltpu.make_async_remote_copy(
                src_ref=src_of(lax.rem(pos + d, count)),
                dst_ref=dst.at[to_or_from],
                send_sem=a_s.at[phase, d],
                recv_sem=a_r.at[phase, d],
                device_id={axis: lax.rem(pos + d, count)},
                device_id_type=MESH,
            )
        sent = [copy(d, pos) for d in range(1, count)]
        for c in sent:
            c.start()
        dst[pos] = src_of(pos)[...]
        return sent, [copy(d, lax.rem(pos + count - d, count)) for d in range(1, count)]

    s1, r1 = exchange(0, "gy", gy, NGY, lambda j: t1.at[j], b1)

    for c in loads:
        c.wait()

    def quarter(z, carry):
        q[z] = q[z] * 0.25
        return carry

    lane = lax.broadcasted_iota(jnp.int32, (CX, 128), 1)

    def pack_xy(k, f):
        px[k, 0] = f[:, PAD, :]
        px[k, 1] = f[:, PAD + CX - 1, :]
        packed = jnp.zeros((CX, 128), F32)
        for z in range(CZ):
            left = pltpu.roll(f[z, pl.ds(PAD, CX), 0:128], z, 1) if z else f[z, pl.ds(PAD, CX), 0:128]
            packed = jnp.where(lane == z, left, packed)
            right = pltpu.roll(f[z, pl.ds(PAD, CX), 128:256], 9 + z, 1)
            packed = jnp.where(lane == 8 + z, right, packed)
        turned = jnp.transpose(packed)
        py[k, 0] = turned[0:8]
        py[k, 1] = turned[8:16]
        for d in (0, 1):
            send(1, k, d, px.at[k, d])
            send(2, k, d, py.at[k, d])

    pack_xy(0, fa)
    lax.fori_loop(0, CZ, quarter, 0)

    for c in r1:
        c.wait_recv()
    s2, r2 = exchange(1, "gx", gx, NGX, lambda j: b1.at[:, j], b2)
    for c in r2:
        c.wait_recv()
    b2v = b2.reshape(NGX * NGY, NT_AX, 128)
    for j in range(NT_AX):
        b3[j] = b2v[:, j, :]
    s3, r3 = exchange(2, "trace", t, NT_AX, lambda j: b3.at[j], b4)
    for c in r3:
        c.wait_recv()

    nodes = b4[...].reshape(n_dev, 128)
    turned = jnp.transpose(nodes)
    row_of = []
    for j in range(CAP):
        zrow = turned[16 * j:16 * j + 1]
        xrow = turned[16 * j + 1:16 * j + 2]
        row_of.append((zrow * float(CX) + xrow).astype(jnp.int32))

    def fill_rows(z, carry):
        here = lax.broadcasted_iota(jnp.int32, (CX, 128), 0) + z * CX
        for j in range(CAP):
            rows_1h[pl.ds(pl.multiple_of(z * CX, CX), CX), j * 128:(j + 1) * 128] = jnp.where(
                here == row_of[j], 1.0, 0.0
            ).astype(BF16)
        return carry

    lax.fori_loop(0, CZ, fill_rows, 0)
    col_iota = lax.broadcasted_iota(jnp.int32, (n_dev, CY), 1)
    for j in range(CAP):
        ycol = nodes[:, 16 * j + 2:16 * j + 3].astype(jnp.int32)
        at_col = col_iota == ycol
        for s in range(STEPS):
            for v, off in ((v_hi, 3), (v_lo, 7)):
                v[s, j * 128:(j + 1) * 128, :] = jnp.where(
                    at_col, nodes[:, 16 * j + off + s:16 * j + off + s + 1], 0.0
                ).astype(BF16)

    def make_source(s):
        def one(z, carry):
            r = rows_1h[pl.ds(pl.multiple_of(z * CX, CX), CX), :]
            s_ref[z] = jnp.dot(r, v_hi[s], preferred_element_type=F32) + jnp.dot(
                r, v_lo[s], preferred_element_type=F32
            )
            return carry
        lax.fori_loop(0, CZ, one, 0)

    lane_r = lax.broadcasted_iota(jnp.int32, (ROWS, 128), 1)
    first, last = lane_r == 0, lane_r == 127

    def plane(k, cur, nxt, z, below, above):
        for r0 in range(0, CX, ROWS):
            rows = pl.ds(PAD + r0, ROWS)
            flat = pl.ds(r0, ROWS)
            h = hy[flat, :]
            h_lo = pltpu.roll(h, lax.rem(128 - z, 128), 1)
            h_hi = pltpu.roll(h, 119 - z, 1)
            mid = []
            for half in (0, 1):
                cols = slice(128 * half, 128 * half + 128)
                mid.append(cur[z, rows, cols])
            fwd = [pltpu.roll(m, 1, 1) for m in mid]
            bwd = [pltpu.roll(m, 127, 1) for m in mid]
            ym = [jnp.where(first, h_lo, fwd[0]), jnp.where(first, fwd[0], fwd[1])]
            yp = [jnp.where(last, bwd[1], bwd[0]), jnp.where(last, h_hi, bwd[1])]
            for half in (0, 1):
                cols = slice(128 * half, 128 * half + 128)
                beside = below(rows, flat, cols) + above(rows, flat, cols)
                beside = beside + (
                    cur[z, pl.ds(PAD + r0 - 1, ROWS), cols] + cur[z, pl.ds(PAD + r0 + 1, ROWS), cols]
                )
                beside = beside + (ym[half] + yp[half])
                m = mid[half]
                nxt[z, rows, cols] = (
                    2.0 * m
                    - nxt[z, rows, cols]
                    + q[z, flat, cols] * (beside - 6.0 * m + s_ref[z, flat, cols])
                )

    bufs = (fa, fb)
    outs = []
    make_source(0)
    for k in range(STEPS):
        cur, nxt = bufs[k % 2], bufs[(k + 1) % 2]
        wait_ghost(1, k)
        wait_ghost(2, k)
        cur[:, PAD - 1, :] = gx_buf[k, 0]
        cur[:, PAD + CX, :] = gx_buf[k, 1]
        both = jnp.concatenate(
            [gy_buf[k, 0], gy_buf[k, 1], jnp.zeros((112, CX), F32)], axis=0
        )
        hy[...] = jnp.transpose(both)

        def inner(z, carry, k=k, cur=cur, nxt=nxt):
            plane(
                k, cur, nxt, z,
                lambda rows, flat, cols: cur[z - 1, rows, cols],
                lambda rows, flat, cols: cur[z + 1, rows, cols],
            )
            return carry

        lax.fori_loop(1, CZ - 1, inner, 0)
        wait_ghost(0, k)
        if k >= 2:
            wait_sent(0, k - 1)
        plane(
            k, cur, nxt, 0,
            lambda rows, flat, cols: gz[k, 0, flat, cols],
            lambda rows, flat, cols: cur[1, rows, cols],
        )
        if k < STEPS - 1:
            send(0, k + 1, 0, nxt.at[0, pl.ds(PAD, CX), :])
        plane(
            k, cur, nxt, CZ - 1,
            lambda rows, flat, cols: cur[CZ - 2, rows, cols],
            lambda rows, flat, cols: gz[k, 1, flat, cols],
        )
        if k < STEPS - 1:
            send(0, k + 1, 1, nxt.at[CZ - 1, pl.ds(PAD, CX), :])
            pack_xy(k + 1, nxt)
            make_source(k + 1)
        if k == STEPS - 2:
            outs.append(pltpu.make_async_copy(nxt.at[:, pl.ds(PAD, CX), :], outp_hbm, osem.at[0]))
            outs[-1].start()
    outs.append(pltpu.make_async_copy(nxt.at[:, pl.ds(PAD, CX), :], outn_hbm, osem.at[1]))
    outs[-1].start()
    for c in s1 + s2 + s3:
        c.wait_send()
    for k in range(STEPS):
        for kind in range(3):
            if kind or k in (0, STEPS - 1):
                wait_sent(kind, k)
    for c in outs:
        c.wait()


def body(traces, coupling, tap_shift, node_tile, node_cell, field_prev, field_now, speed_sq):
    combined = jnp.sum(traces.astype(F32) * coupling.astype(F32)[:, :, None], axis=1)
    field = jax.ShapeDtypeStruct((CZ, CX, CY), F32)
    vmem = pl.BlockSpec(memory_space=pltpu.VMEM)
    hbm = pl.BlockSpec(memory_space=pl.ANY)
    dma = pltpu.SemaphoreType.DMA
    return pl.pallas_call(
        kernel,
        out_shape=(field, field),
        in_specs=[vmem] * 5 + [hbm] * 3,
        out_specs=(hbm, hbm),
        scratch_shapes=[
            pltpu.VMEM((CZ, CX + 2 * PAD, CY), F32),
            pltpu.VMEM((CZ, CX + 2 * PAD, CY), F32),
            pltpu.VMEM((CZ, CX, CY), F32),
            pltpu.VMEM((CZ, CX, CY), F32),
            pltpu.VMEM((STEPS, 2, CX, CY), F32),
            pltpu.VMEM((STEPS, 2, CZ, CY), F32),
            pltpu.VMEM((STEPS, 2, CZ, CX), F32),
            pltpu.VMEM((STEPS, 2, CZ, CY), F32),
            pltpu.VMEM((STEPS, 2, CZ, CX), F32),
            pltpu.VMEM((CX, 128), F32),
            pltpu.VMEM((CZ * CX, CAP * 128), BF16),
            pltpu.VMEM((STEPS, CAP * 128, CY), BF16),
            pltpu.VMEM((STEPS, CAP * 128, CY), BF16),
            pltpu.VMEM((NGY, NGX, NT_AX, 128), F32),
            pltpu.VMEM((NGY, NGX, NT_AX, 128), F32),
            pltpu.VMEM((NGX, NGY, NT_AX, 128), F32),
            pltpu.VMEM((NT_AX, NGX * NGY, 128), F32),
            pltpu.VMEM((NT_AX, NGX * NGY, 128), F32),
            dma((3,)),
            dma((2,)),
            dma((STEPS, 2)),
            dma((STEPS, 2)),
            dma((STEPS, 2)),
            dma((STEPS, 2)),
            dma((STEPS, 2)),
            dma((STEPS, 2)),
            dma((3, NT_AX)),
            dma((3, NT_AX)),
        ],
        compiler_params=pltpu.CompilerParams(collective_id=0, has_side_effects=True),
    )(
        combined,
        jnp.asarray(window_table()),
        tap_shift.reshape(1, -1),
        node_tile.reshape(1, -1),
        node_cell.reshape(1, -1),
        field_prev,
        field_now,
        speed_sq,
    )


def solution(mesh):
    everywhere = ("trace", "gx", "gy")
    placed = (
        P(everywhere, None, None),
        P(everywhere, None),
        P(everywhere),
        P(everywhere, None),
        P(everywhere),
        P("trace", "gx", "gy"),
        P("trace", "gx", "gy"),
        P("trace", "gx", "gy"),
    )
    return jax.shard_map(
        body,
        mesh=mesh,
        in_specs=placed,
        out_specs=(P("trace", "gx", "gy"), P("trace", "gx", "gy")),
        check_vma=False,
    )
```

```python
import math

import jax
import jax.numpy as jnp
import numpy as np
from jax import lax
from jax.experimental import pallas as pl
from jax.experimental.pallas import tpu as pltpu
from jax.sharding import PartitionSpec as P

NT = 256
STEPS = 4
RATE = 64
CZ, CX, CY = 8, 256, 256
NT_AX, NGX, NGY = 8, 4, 4
CAP = 4
COMP = 4
PAD = 8
ROWS = 32
MESH = pl.DeviceIdType.MESH
F32 = jnp.float32
BF16 = jnp.bfloat16


def window_table():
    u = (np.arange(NT)[None, :] + np.arange(NT)[:, None] - (NT - RATE // 2)).astype(np.float64)
    w = np.sinc(u / RATE) * 0.5 * (1.0 + np.cos(math.pi * u / (2.0 * RATE)))
    return np.where(np.abs(u) < 2.0 * RATE, w, 0.0).astype(np.float32)


def nt_dot(a, b, precision=None):
    return lax.dot_general(
        a, b, (((1,), (1,)), ((), ())), precision=precision, preferred_element_type=F32
    )


def kernel(
    traces_hbm, coup_ref, win_ref, shift_ref, tile_ref, cell_ref, prev_hbm, now_hbm, speed_hbm,
    outp_ref, outn_ref,
    tr, fa, fb, q, s_ref, gz, gx_buf, gy_buf, px, py, hy, rows_1h, v_hi, v_lo, t1, b4,
    lsem, osem, zs, zr, xs, xr, ys, yr, a_s, a_r,
):
    t = lax.axis_index("trace")
    gx = lax.axis_index("gx")
    gy = lax.axis_index("gy")
    n_dev = NT_AX * NGX * NGY
    me = (t * NGX + gx) * NGY + gy

    load_tr = pltpu.make_async_copy(traces_hbm, tr, lsem.at[3])
    load_tr.start()
    loads = [
        pltpu.make_async_copy(now_hbm, fa.at[:, pl.ds(PAD, CX), :], lsem.at[0]),
        pltpu.make_async_copy(prev_hbm, fb.at[:, pl.ds(PAD, CX), :], lsem.at[1]),
        pltpu.make_async_copy(speed_hbm, q, lsem.at[2]),
    ]
    for c in loads:
        c.start()

    def peer(d):
        k = lax.rem(me + d, n_dev)
        return k, (k // (NGX * NGY), lax.rem(k // NGY, NGX), lax.rem(k, NGY))

    barrier = pltpu.get_barrier_semaphore()

    def greet(d, carry):
        _, where = peer(d)
        pl.semaphore_signal(barrier, inc=1, device_id=where, device_id_type=MESH)
        return carry

    lax.fori_loop(1, n_dev, greet, 0)

    sides = (("trace", t, NT_AX), ("gx", gx, NGX), ("gy", gy, NGY))
    for buf, (_, pos, count) in zip((gz, gx_buf, gy_buf), sides):
        for side in (0, 1):
            @pl.when(pos == (0 if side == 0 else count - 1))
            def _(buf=buf, side=side):
                for k in range(STEPS):
                    buf[k, side] = jnp.zeros(buf.shape[2:], F32)

    def halo(kind, k, d, src=None):
        axis, pos, count = sides[kind]
        ghost = (gz, gx_buf, gy_buf)[kind]
        ssem, rsem = ((zs, zr), (xs, xr), (ys, yr))[kind]
        if src is None:
            src = ghost.at[k, 1 - d]
        to = jnp.maximum(pos - 1, 0) if d == 0 else jnp.minimum(pos + 1, count - 1)
        return pltpu.make_async_remote_copy(
            src_ref=src,
            dst_ref=ghost.at[k, 1 - d],
            send_sem=ssem.at[k, d],
            recv_sem=rsem.at[k, 1 - d],
            device_id={axis: to},
            device_id_type=MESH,
        )

    def exists(kind, d):
        _, pos, count = sides[kind]
        return pos > 0 if d == 0 else pos < count - 1

    def send(kind, k, d, src):
        @pl.when(exists(kind, d))
        def _():
            halo(kind, k, d, src).start()

    def wait_ghost(kind, k):
        for side in (0, 1):
            @pl.when(exists(kind, side))
            def _(side=side):
                halo(kind, k, 1 - side).wait_recv()

    def wait_sent(kind, k):
        for d in (0, 1):
            @pl.when(exists(kind, d))
            def _(d=d):
                halo(kind, k, d).wait_send()

    coup = jnp.transpose(
        jnp.concatenate([coup_ref[...].astype(F32), jnp.zeros((128 - COMP, NT), F32)], axis=0)
    )
    lane_i = lax.broadcasted_iota(jnp.int32, (NT, 128), 1)
    node_i = lax.broadcasted_iota(jnp.int32, (NT, 128), 0)
    comp = lane_i % COMP
    weight = coup[:, COMP - 1:COMP]
    for c in range(COMP - 2, -1, -1):
        weight = jnp.where(comp == c, coup[:, c:c + 1], weight)
    weight = jnp.where(lane_i // COMP == node_i % 32, weight, 0.0).astype(BF16)
    load_tr.wait()
    flat_tr = tr.reshape(NT * COMP, NT)
    combined = jnp.concatenate(
        [
            jnp.dot(
                weight[b * 32:(b + 1) * 32, :], flat_tr[b * 128:(b + 1) * 128, :],
                preferred_element_type=F32,
            )
            for b in range(NT // 32)
        ],
        axis=0,
    )

    at = nt_dot(win_ref[...], combined, lax.Precision.HIGHEST)
    shift = shift_ref[...]
    picked = lax.broadcasted_iota(jnp.int32, (RATE, NT), 0) == shift
    amps = [
        jnp.sum(jnp.where(picked, at[s * RATE:(s + 1) * RATE, :], 0.0), axis=0, keepdims=True)
        for s in range(STEPS)
    ]
    cell = cell_ref[...]
    cz = (cell // (CX * CY)).astype(F32)
    cx = ((cell // CY) % CX).astype(F32)
    cy = (cell % CY).astype(F32)
    hi = [a.astype(BF16).astype(F32) for a in amps]
    lo = [a - h for a, h in zip(amps, hi)]
    zero_row = jnp.zeros((1, NT), F32)
    vals = jnp.concatenate([cz, cx, cy] + hi + lo + [zero_row] * 5, axis=0).astype(BF16)
    onehot = lax.broadcasted_iota(jnp.int32, (n_dev, NT), 0) == tile_ref[...]
    onehot_f = jnp.where(onehot, 1.0, 0.0)
    before = jnp.where(
        lax.broadcasted_iota(jnp.int32, (NT, NT), 0) < lax.broadcasted_iota(jnp.int32, (NT, NT), 1),
        1.0, 0.0,
    ).astype(BF16)
    rank = jnp.dot(onehot_f.astype(BF16), before, preferred_element_type=F32)
    table = jnp.zeros((n_dev, 128), F32)
    for j in range(CAP):
        picks = jnp.where(rank == float(j), onehot_f, 0.0).astype(BF16)
        parts = []
        if j:
            parts.append(jnp.zeros((16 * j, NT), BF16))
        parts.append(vals)
        parts.append(jnp.zeros((128 - 16 * (j + 1), NT), BF16))
        table = table + nt_dot(picks, jnp.concatenate(parts, axis=0))
    t1[...] = table.reshape(n_dev, 1, 128)

    pl.semaphore_wait(barrier, n_dev - 1)

    def post(d, carry):
        k, where = peer(d)
        pltpu.make_async_remote_copy(
            src_ref=t1.at[k],
            dst_ref=b4.at[me],
            send_sem=a_s.at[0],
            recv_sem=a_r.at[0],
            device_id=where,
            device_id_type=MESH,
        ).start()
        return carry

    lax.fori_loop(1, n_dev, post, 0)
    b4[me] = t1[me]
    all_rows = pltpu.make_async_remote_copy(
        src_ref=t1.at[pl.ds(0, n_dev - 1)],
        dst_ref=b4.at[pl.ds(0, n_dev - 1)],
        send_sem=a_s.at[0],
        recv_sem=a_r.at[0],
        device_id=peer(1)[1],
        device_id_type=MESH,
    )

    send(0, 0, 0, now_hbm.at[0])
    send(0, 0, 1, now_hbm.at[CZ - 1])

    lane = lax.broadcasted_iota(jnp.int32, (CX, 128), 1)

    def pack_xy(k, f):
        px[k, 0] = f[:, PAD, :]
        px[k, 1] = f[:, PAD + CX - 1, :]
        packed = jnp.zeros((CX, 128), F32)
        for z in range(CZ):
            left = pltpu.roll(f[z, pl.ds(PAD, CX), 0:128], z, 1) if z else f[z, pl.ds(PAD, CX), 0:128]
            packed = jnp.where(lane == z, left, packed)
            right = pltpu.roll(f[z, pl.ds(PAD, CX), 128:256], 9 + z, 1)
            packed = jnp.where(lane == 8 + z, right, packed)
        turned = jnp.transpose(packed)
        py[k, 0] = turned[0:8]
        py[k, 1] = turned[8:16]
        for d in (0, 1):
            send(1, k, d, px.at[k, d])
            send(2, k, d, py.at[k, d])

    for c in loads:
        c.wait()
    pack_xy(0, fa)

    def quarter(z, carry):
        q[z] = q[z] * 0.25
        return carry

    lax.fori_loop(0, CZ, quarter, 0)

    def make_source(s):
        def one(i, carry):
            r = rows_1h[pl.ds(pl.multiple_of(i * 2 * CX, 2 * CX), 2 * CX), :]
            total = jnp.dot(r, v_hi[s], preferred_element_type=F32) + jnp.dot(
                r, v_lo[s], preferred_element_type=F32
            )
            s_ref[pl.ds(i * 2, 2)] = total.reshape(2, CX, CY)
            return carry
        lax.fori_loop(0, CZ // 2, one, 0)

    lane_r = lax.broadcasted_iota(jnp.int32, (ROWS, 128), 1)
    first, last = lane_r == 0, lane_r == 127

    def plane(cur, old, dst, dst_pad, z, below, above, source):
        for r0 in range(0, CX, ROWS):
            rows = pl.ds(PAD + r0, ROWS)
            flat = pl.ds(r0, ROWS)
            h = hy[flat, :]
            h_lo = pltpu.roll(h, lax.rem(128 - z, 128), 1)
            h_hi = pltpu.roll(h, 119 - z, 1)
            mid = []
            for half in (0, 1):
                cols = slice(128 * half, 128 * half + 128)
                mid.append(cur[z, rows, cols])
            fwd = [pltpu.roll(m, 1, 1) for m in mid]
            bwd = [pltpu.roll(m, 127, 1) for m in mid]
            ym = [jnp.where(first, h_lo, fwd[0]), jnp.where(first, fwd[0], fwd[1])]
            yp = [jnp.where(last, bwd[1], bwd[0]), jnp.where(last, h_hi, bwd[1])]
            for half in (0, 1):
                cols = slice(128 * half, 128 * half + 128)
                beside = below(rows, flat, cols) + above(rows, flat, cols)
                beside = beside + (
                    cur[z, pl.ds(PAD + r0 - 1, ROWS), cols] + cur[z, pl.ds(PAD + r0 + 1, ROWS), cols]
                )
                beside = beside + (ym[half] + yp[half])
                m = mid[half]
                beside = beside - 6.0 * m
                if source:
                    beside = beside + s_ref[z, flat, cols]
                dst[z, pl.ds(dst_pad + r0, ROWS), cols] = (
                    2.0 * m - old[z, rows, cols] + q[z, flat, cols] * beside
                )

    def ghosts_xy(k, cur):
        wait_ghost(1, k)
        wait_ghost(2, k)
        cur[:, PAD - 1, :] = gx_buf[k, 0]
        cur[:, PAD + CX, :] = gx_buf[k, 1]
        both = jnp.concatenate(
            [gy_buf[k, 0], gy_buf[k, 1], jnp.zeros((112, CX), F32)], axis=0
        )
        hy[...] = jnp.transpose(both)

    def inner_planes(cur, old, dst, dst_pad, source):
        def inner(z, carry):
            plane(
                cur, old, dst, dst_pad, z,
                lambda rows, flat, cols: cur[z - 1, rows, cols],
                lambda rows, flat, cols: cur[z + 1, rows, cols],
                source,
            )
            return carry

        lax.fori_loop(1, CZ - 1, inner, 0)

    def low_plane(k, cur, old, dst, dst_pad, source):
        plane(
            cur, old, dst, dst_pad, 0,
            lambda rows, flat, cols: gz[k, 0, flat, cols],
            lambda rows, flat, cols: cur[1, rows, cols],
            source,
        )

    def high_plane(k, cur, old, dst, dst_pad, source):
        plane(
            cur, old, dst, dst_pad, CZ - 1,
            lambda rows, flat, cols: cur[CZ - 2, rows, cols],
            lambda rows, flat, cols: gz[k, 1, flat, cols],
            source,
        )

    ghosts_xy(0, fa)
    inner_planes(fa, fb, fb, PAD, False)
    wait_ghost(0, 0)
    low_plane(0, fa, fb, fb, PAD, False)
    high_plane(0, fa, fb, fb, PAD, False)

    all_rows.wait_recv()

    nodes = b4[...].reshape(n_dev, 128)
    turned = jnp.transpose(nodes)
    row_of = []
    for j in range(CAP):
        zrow = turned[16 * j:16 * j + 1]
        xrow = turned[16 * j + 1:16 * j + 2]
        row_of.append((zrow * float(CX) + xrow).astype(jnp.int32))

    def fill_rows(z, carry):
        here = lax.broadcasted_iota(jnp.int32, (CX, 128), 0) + z * CX
        for j in range(CAP):
            rows_1h[pl.ds(pl.multiple_of(z * CX, CX), CX), j * 128:(j + 1) * 128] = jnp.where(
                here == row_of[j], 1.0, 0.0
            ).astype(BF16)
        return carry

    lax.fori_loop(0, CZ, fill_rows, 0)
    col_iota = lax.broadcasted_iota(jnp.int32, (n_dev, CY), 1)
    for j in range(CAP):
        ycol = nodes[:, 16 * j + 2:16 * j + 3].astype(jnp.int32)
        at_col = col_iota == ycol
        for s in range(STEPS):
            for v, off in ((v_hi, 3), (v_lo, 7)):
                v[s, j * 128:(j + 1) * 128, :] = jnp.where(
                    at_col, nodes[:, 16 * j + off + s:16 * j + off + s + 1], 0.0
                ).astype(BF16)

    make_source(0)

    def add_source(z, carry):
        rows = pl.ds(PAD, CX)
        fb[z, rows, :] = fb[z, rows, :] + q[z] * s_ref[z]
        return carry

    def send_z(k, f):
        send(0, k, 0, f.at[0, pl.ds(PAD, CX), :])
        send(0, k, 1, f.at[CZ - 1, pl.ds(PAD, CX), :])

    add_source(0, 0)
    add_source(CZ - 1, 0)
    send_z(1, fb)
    lax.fori_loop(1, CZ - 1, add_source, 0)
    pack_xy(1, fb)
    make_source(1)

    for k, cur, nxt in ((1, fb, fa), (2, fa, fb)):
        ghosts_xy(k, cur)
        inner_planes(cur, nxt, nxt, PAD, True)
        wait_ghost(0, k)
        if k >= 2:
            wait_sent(0, k - 1)
        low_plane(k, cur, nxt, nxt, PAD, True)
        high_plane(k, cur, nxt, nxt, PAD, True)
        send_z(k + 1, nxt)
        pack_xy(k + 1, nxt)
        make_source(k + 1)

    copy_prev = pltpu.make_async_copy(fb.at[:, pl.ds(PAD, CX), :], outp_ref, osem.at[0])
    copy_prev.start()
    ghosts_xy(3, fb)
    inner_planes(fb, fa, outn_ref, 0, True)
    wait_ghost(0, 3)
    low_plane(3, fb, fa, outn_ref, 0, True)
    high_plane(3, fb, fa, outn_ref, 0, True)

    all_rows.wait_send()
    for k in range(STEPS):
        for kind in range(3):
            if kind or k != 1:
                wait_sent(kind, k)
    copy_prev.wait()


def body(traces, coupling, tap_shift, node_tile, node_cell, field_prev, field_now, speed_sq):
    vmem = pl.BlockSpec(memory_space=pltpu.VMEM)
    hbm = pl.BlockSpec(memory_space=pltpu.HBM)
    dma = pltpu.SemaphoreType.DMA
    n_dev = NT_AX * NGX * NGY
    return pl.pallas_call(
        kernel,
        out_shape=(pltpu.VMEM((CZ, CX, CY), F32), pltpu.VMEM((CZ, CX, CY), F32)),
        in_specs=[hbm] + [vmem] * 5 + [hbm] * 3,
        out_specs=(vmem, vmem),
        scratch_shapes=[
            pltpu.VMEM((NT, COMP, NT), BF16),
            pltpu.VMEM((CZ, CX + 2 * PAD, CY), F32),
            pltpu.VMEM((CZ, CX + 2 * PAD, CY), F32),
            pltpu.VMEM((CZ, CX, CY), F32),
            pltpu.VMEM((CZ, CX, CY), F32),
            pltpu.VMEM((STEPS, 2, CX, CY), F32),
            pltpu.VMEM((STEPS, 2, CZ, CY), F32),
            pltpu.VMEM((STEPS, 2, CZ, CX), F32),
            pltpu.VMEM((STEPS, 2, CZ, CY), F32),
            pltpu.VMEM((STEPS, 2, CZ, CX), F32),
            pltpu.VMEM((CX, 128), F32),
            pltpu.VMEM((CZ * CX, CAP * 128), BF16),
            pltpu.VMEM((STEPS, CAP * 128, CY), BF16),
            pltpu.VMEM((STEPS, CAP * 128, CY), BF16),
            pltpu.VMEM((n_dev, 1, 128), F32),
            pltpu.VMEM((n_dev, 1, 128), F32),
            dma((4,)),
            dma((1,)),
            dma((STEPS, 2)),
            dma((STEPS, 2)),
            dma((STEPS, 2)),
            dma((STEPS, 2)),
            dma((STEPS, 2)),
            dma((STEPS, 2)),
            dma((1,)),
            dma((1,)),
        ],
        compiler_params=pltpu.CompilerParams(
            collective_id=0, has_side_effects=True, vmem_limit_bytes=62_400_000
        ),
    )(
        traces,
        coupling.T,
        jnp.asarray(window_table()),
        tap_shift.reshape(1, -1),
        node_tile.reshape(1, -1),
        node_cell.reshape(1, -1),
        field_prev,
        field_now,
        speed_sq,
    )


def solution(mesh):
    everywhere = ("trace", "gx", "gy")
    placed = (
        P(everywhere, None, None),
        P(everywhere, None),
        P(everywhere),
        P(everywhere, None),
        P(everywhere),
        P("trace", "gx", "gy"),
        P("trace", "gx", "gy"),
        P("trace", "gx", "gy"),
    )
    return jax.shard_map(
        body,
        mesh=mesh,
        in_specs=placed,
        out_specs=(P("trace", "gx", "gy"), P("trace", "gx", "gy")),
        check_vma=False,
    )
```

```python
import math

import jax
import jax.numpy as jnp
import numpy as np
from jax import lax
from jax.experimental import pallas as pl
from jax.experimental.pallas import tpu as pltpu
from jax.sharding import PartitionSpec as P

NT = 256
STEPS = 4
RATE = 64
CZ, CX, CY = 8, 256, 256
NT_AX, NGX, NGY = 8, 4, 4
CAP = 4
COMP = 4
PAD = 8
ROWS = 32
MESH = pl.DeviceIdType.MESH
F32 = jnp.float32
BF16 = jnp.bfloat16


def window_table():
    u = (np.arange(NT)[None, :] + np.arange(NT)[:, None] - (NT - RATE // 2)).astype(np.float64)
    w = np.sinc(u / RATE) * 0.5 * (1.0 + np.cos(math.pi * u / (2.0 * RATE)))
    return np.where(np.abs(u) < 2.0 * RATE, w, 0.0).astype(np.float32)


def nt_dot(a, b, precision=None):
    return lax.dot_general(
        a, b, (((1,), (1,)), ((), ())), precision=precision, preferred_element_type=F32
    )


def kernel(
    traces_hbm, coup_ref, win_ref, shift_ref, tile_ref, cell_ref, prev_hbm, now_hbm, speed_hbm,
    outp_ref, outn_ref,
    tr, fa, fb, q, s_ref, gz, gx_buf, gy_buf, px, py, hy, rows_1h, v_hi, v_lo, t1, b4, dense,
    lsem, osem, zs, zr, xs, xr, ys, yr, a_s, a_r,
):
    t = lax.axis_index("trace")
    gx = lax.axis_index("gx")
    gy = lax.axis_index("gy")
    n_dev = NT_AX * NGX * NGY
    me = (t * NGX + gx) * NGY + gy

    load_tr = pltpu.make_async_copy(traces_hbm, tr, lsem.at[3])
    load_tr.start()
    loads = [
        pltpu.make_async_copy(now_hbm, fa.at[:, pl.ds(PAD, CX), :], lsem.at[0]),
        pltpu.make_async_copy(prev_hbm, fb.at[:, pl.ds(PAD, CX), :], lsem.at[1]),
        pltpu.make_async_copy(speed_hbm, q, lsem.at[2]),
    ]
    for c in loads:
        c.start()

    def peer(d):
        k = lax.rem(me + d, n_dev)
        return k, (k // (NGX * NGY), lax.rem(k // NGY, NGX), lax.rem(k, NGY))

    barrier = pltpu.get_barrier_semaphore()

    def greet(d, carry):
        _, where = peer(d)
        pl.semaphore_signal(barrier, inc=1, device_id=where, device_id_type=MESH)
        return carry

    lax.fori_loop(1, n_dev, greet, 0)

    sides = (("trace", t, NT_AX), ("gx", gx, NGX), ("gy", gy, NGY))
    for buf, (_, pos, count) in zip((gz, gx_buf, gy_buf), sides):
        for side in (0, 1):
            @pl.when(pos == (0 if side == 0 else count - 1))
            def _(buf=buf, side=side):
                for k in range(STEPS):
                    buf[k, side] = jnp.zeros(buf.shape[2:], F32)

    def halo(kind, k, d, src=None):
        axis, pos, count = sides[kind]
        ghost = (gz, gx_buf, gy_buf)[kind]
        ssem, rsem = ((zs, zr), (xs, xr), (ys, yr))[kind]
        if src is None:
            src = ghost.at[k, 1 - d]
        to = jnp.maximum(pos - 1, 0) if d == 0 else jnp.minimum(pos + 1, count - 1)
        return pltpu.make_async_remote_copy(
            src_ref=src,
            dst_ref=ghost.at[k, 1 - d],
            send_sem=ssem.at[k, d],
            recv_sem=rsem.at[k, 1 - d],
            device_id={axis: to},
            device_id_type=MESH,
        )

    def exists(kind, d):
        _, pos, count = sides[kind]
        return pos > 0 if d == 0 else pos < count - 1

    def send(kind, k, d, src):
        @pl.when(exists(kind, d))
        def _():
            halo(kind, k, d, src).start()

    def wait_ghost(kind, k):
        for side in (0, 1):
            @pl.when(exists(kind, side))
            def _(side=side):
                halo(kind, k, 1 - side).wait_recv()

    def wait_sent(kind, k):
        for d in (0, 1):
            @pl.when(exists(kind, d))
            def _(d=d):
                halo(kind, k, d).wait_send()

    coup = jnp.transpose(
        jnp.concatenate([coup_ref[...].astype(F32), jnp.zeros((128 - COMP, NT), F32)], axis=0)
    )
    lane_i = lax.broadcasted_iota(jnp.int32, (NT, 128), 1)
    node_i = lax.broadcasted_iota(jnp.int32, (NT, 128), 0)
    comp = lane_i % COMP
    weight = coup[:, COMP - 1:COMP]
    for c in range(COMP - 2, -1, -1):
        weight = jnp.where(comp == c, coup[:, c:c + 1], weight)
    weight = jnp.where(lane_i // COMP == node_i % 32, weight, 0.0).astype(BF16)
    load_tr.wait()
    flat_tr = tr.reshape(NT * COMP, NT)
    combined = jnp.concatenate(
        [
            jnp.dot(
                weight[b * 32:(b + 1) * 32, :], flat_tr[b * 128:(b + 1) * 128, :],
                preferred_element_type=F32,
            )
            for b in range(NT // 32)
        ],
        axis=0,
    )

    at = nt_dot(win_ref[...], combined, lax.Precision.HIGHEST)
    shift = shift_ref[...]
    picked = lax.broadcasted_iota(jnp.int32, (RATE, NT), 0) == shift
    amps = [
        jnp.sum(jnp.where(picked, at[s * RATE:(s + 1) * RATE, :], 0.0), axis=0, keepdims=True)
        for s in range(STEPS)
    ]
    cell = cell_ref[...]
    cz = (cell // (CX * CY)).astype(F32)
    cx = ((cell // CY) % CX).astype(F32)
    cy = (cell % CY).astype(F32)
    hi = [a.astype(BF16).astype(F32) for a in amps]
    lo = [a - h for a, h in zip(amps, hi)]
    zero_row = jnp.zeros((1, NT), F32)
    vals = jnp.concatenate([cz, cx, cy] + hi + lo + [zero_row] * 5, axis=0).astype(BF16)
    onehot = lax.broadcasted_iota(jnp.int32, (n_dev, NT), 0) == tile_ref[...]
    onehot_f = jnp.where(onehot, 1.0, 0.0)
    before = jnp.where(
        lax.broadcasted_iota(jnp.int32, (NT, NT), 0) < lax.broadcasted_iota(jnp.int32, (NT, NT), 1),
        1.0, 0.0,
    ).astype(BF16)
    rank = jnp.dot(onehot_f.astype(BF16), before, preferred_element_type=F32)
    table = jnp.zeros((n_dev, 128), F32)
    for j in range(CAP):
        picks = jnp.where(rank == float(j), onehot_f, 0.0).astype(BF16)
        parts = []
        if j:
            parts.append(jnp.zeros((16 * j, NT), BF16))
        parts.append(vals)
        parts.append(jnp.zeros((128 - 16 * (j + 1), NT), BF16))
        table = table + nt_dot(picks, jnp.concatenate(parts, axis=0))
    t1[...] = table.reshape(n_dev, 1, 128)

    pl.semaphore_wait(barrier, n_dev - 1)

    def post(d, carry):
        k, where = peer(d)
        pltpu.make_async_remote_copy(
            src_ref=t1.at[k],
            dst_ref=b4.at[me],
            send_sem=a_s.at[0],
            recv_sem=a_r.at[0],
            device_id=where,
            device_id_type=MESH,
        ).start()
        return carry

    lax.fori_loop(1, n_dev, post, 0)
    b4[me] = t1[me]
    all_rows = pltpu.make_async_remote_copy(
        src_ref=t1.at[pl.ds(0, n_dev - 1)],
        dst_ref=b4.at[pl.ds(0, n_dev - 1)],
        send_sem=a_s.at[0],
        recv_sem=a_r.at[0],
        device_id=peer(1)[1],
        device_id_type=MESH,
    )

    send(0, 0, 0, now_hbm.at[0])
    send(0, 0, 1, now_hbm.at[CZ - 1])

    lane = lax.broadcasted_iota(jnp.int32, (CX, 128), 1)

    def pack_xy(k, f):
        px[k, 0] = f[:, PAD, :]
        px[k, 1] = f[:, PAD + CX - 1, :]
        packed = jnp.zeros((CX, 128), F32)
        for z in range(CZ):
            left = pltpu.roll(f[z, pl.ds(PAD, CX), 0:128], z, 1) if z else f[z, pl.ds(PAD, CX), 0:128]
            packed = jnp.where(lane == z, left, packed)
            right = pltpu.roll(f[z, pl.ds(PAD, CX), 128:256], 9 + z, 1)
            packed = jnp.where(lane == 8 + z, right, packed)
        turned = jnp.transpose(packed)
        py[k, 0] = turned[0:8]
        py[k, 1] = turned[8:16]
        for d in (0, 1):
            send(1, k, d, px.at[k, d])
            send(2, k, d, py.at[k, d])

    for c in loads:
        c.wait()
    pack_xy(0, fa)

    def quarter(z, carry):
        q[z] = q[z] * 0.25
        return carry

    lax.fori_loop(0, CZ, quarter, 0)

    def scattered(s, r):
        total = jnp.dot(r, v_hi[s], preferred_element_type=F32) + jnp.dot(
            r, v_lo[s], preferred_element_type=F32
        )
        return total.reshape(2, CX, CY)

    def source_ends(s):
        both = scattered(s, jnp.concatenate([rows_1h[0:CX], rows_1h[(CZ - 1) * CX:CZ * CX]], axis=0))
        s_ref[0] = both[0]
        s_ref[CZ - 1] = both[1]

    def source_inner(s):
        def one(i, carry):
            z = 2 * i + 1
            s_ref[pl.ds(z, 2)] = scattered(s, rows_1h[pl.ds(pl.multiple_of(z * CX, CX), 2 * CX), :])
            return carry
        lax.fori_loop(0, CZ // 2 - 1, one, 0)

    def make_source(s):
        source_ends(s)
        source_inner(s)

    lane_r = lax.broadcasted_iota(jnp.int32, (ROWS, 128), 1)
    first, last = lane_r == 0, lane_r == 127

    def plane(cur, old, dst, dst_pad, z, below, above, source):
        for r0 in range(0, CX, ROWS):
            rows = pl.ds(PAD + r0, ROWS)
            flat = pl.ds(r0, ROWS)
            h = hy[flat, :]
            h_lo = pltpu.roll(h, lax.rem(128 - z, 128), 1)
            h_hi = pltpu.roll(h, 119 - z, 1)
            mid = []
            for half in (0, 1):
                cols = slice(128 * half, 128 * half + 128)
                mid.append(cur[z, rows, cols])
            fwd = [pltpu.roll(m, 1, 1) for m in mid]
            bwd = [pltpu.roll(m, 127, 1) for m in mid]
            ym = [jnp.where(first, h_lo, fwd[0]), jnp.where(first, fwd[0], fwd[1])]
            yp = [jnp.where(last, bwd[1], bwd[0]), jnp.where(last, h_hi, bwd[1])]
            for half in (0, 1):
                cols = slice(128 * half, 128 * half + 128)
                beside = below(rows, flat, cols) + above(rows, flat, cols)
                beside = beside + (
                    cur[z, pl.ds(PAD + r0 - 1, ROWS), cols] + cur[z, pl.ds(PAD + r0 + 1, ROWS), cols]
                )
                beside = beside + (ym[half] + yp[half])
                m = mid[half]
                beside = beside - 6.0 * m
                if source:
                    beside = beside + s_ref[z, flat, cols]
                dst[z, pl.ds(dst_pad + r0, ROWS), cols] = (
                    2.0 * m - old[z, rows, cols] + q[z, flat, cols] * beside
                )

    def ghosts_xy(k, cur):
        wait_ghost(1, k)
        wait_ghost(2, k)
        cur[:, PAD - 1, :] = gx_buf[k, 0]
        cur[:, PAD + CX, :] = gx_buf[k, 1]
        both = jnp.concatenate(
            [gy_buf[k, 0], gy_buf[k, 1], jnp.zeros((112, CX), F32)], axis=0
        )
        hy[...] = jnp.transpose(both)

    def inner_planes(cur, old, dst, dst_pad, source):
        def inner(z, carry):
            plane(
                cur, old, dst, dst_pad, z,
                lambda rows, flat, cols: cur[z - 1, rows, cols],
                lambda rows, flat, cols: cur[z + 1, rows, cols],
                source,
            )
            return carry

        lax.fori_loop(1, CZ - 1, inner, 0)

    def low_plane(k, cur, old, dst, dst_pad, source):
        plane(
            cur, old, dst, dst_pad, 0,
            lambda rows, flat, cols: gz[k, 0, flat, cols],
            lambda rows, flat, cols: cur[1, rows, cols],
            source,
        )

    def high_plane(k, cur, old, dst, dst_pad, source):
        plane(
            cur, old, dst, dst_pad, CZ - 1,
            lambda rows, flat, cols: cur[CZ - 2, rows, cols],
            lambda rows, flat, cols: gz[k, 1, flat, cols],
            source,
        )

    ghosts_xy(0, fa)
    inner_planes(fa, fb, fb, PAD, False)
    wait_ghost(0, 0)
    low_plane(0, fa, fb, fb, PAD, False)
    high_plane(0, fa, fb, fb, PAD, False)

    all_rows.wait_recv()

    dense[...] = b4[...].reshape(n_dev, 128)
    nodes = dense[...]
    turned = jnp.transpose(nodes)
    row_of = []
    for j in range(CAP):
        zrow = turned[16 * j:16 * j + 1]
        xrow = turned[16 * j + 1:16 * j + 2]
        row_of.append((zrow * float(CX) + xrow).astype(jnp.int32))

    def fill_rows(z, carry):
        here = lax.broadcasted_iota(jnp.int32, (CX, 128), 0) + z * CX
        for j in range(CAP):
            rows_1h[pl.ds(pl.multiple_of(z * CX, CX), CX), j * 128:(j + 1) * 128] = jnp.where(
                here == row_of[j], 1.0, 0.0
            ).astype(BF16)
        return carry

    col_iota = lax.broadcasted_iota(jnp.int32, (n_dev, CY), 1)

    def fill_values(s_list):
        for j in range(CAP):
            at_col = col_iota == dense[:, 16 * j + 2:16 * j + 3].astype(jnp.int32)
            for s in s_list:
                for v, off in ((v_hi, 3), (v_lo, 7)):
                    c = 16 * j + off + s
                    v[s, j * 128:(j + 1) * 128, :] = jnp.where(
                        at_col, dense[:, c:c + 1], 0.0
                    ).astype(BF16)

    def add_source(z, carry):
        rows = pl.ds(PAD, CX)
        fb[z, rows, :] = fb[z, rows, :] + q[z] * s_ref[z]
        return carry

    def send_z(k, f):
        send(0, k, 0, f.at[0, pl.ds(PAD, CX), :])
        send(0, k, 1, f.at[CZ - 1, pl.ds(PAD, CX), :])

    fill_rows(0, 0)
    fill_rows(CZ - 1, 0)
    fill_values((0,))
    source_ends(0)
    add_source(0, 0)
    add_source(CZ - 1, 0)
    send_z(1, fb)
    lax.fori_loop(1, CZ - 1, fill_rows, 0)
    source_inner(0)
    lax.fori_loop(1, CZ - 1, add_source, 0)
    pack_xy(1, fb)
    fill_values((1, 2, 3))
    make_source(1)

    for k, cur, nxt in ((1, fb, fa), (2, fa, fb)):
        ghosts_xy(k, cur)
        inner_planes(cur, nxt, nxt, PAD, True)
        wait_ghost(0, k)
        if k >= 2:
            wait_sent(0, k - 1)
        low_plane(k, cur, nxt, nxt, PAD, True)
        high_plane(k, cur, nxt, nxt, PAD, True)
        send_z(k + 1, nxt)
        pack_xy(k + 1, nxt)
        make_source(k + 1)

    copy_prev = pltpu.make_async_copy(fb.at[:, pl.ds(PAD, CX), :], outp_ref, osem.at[0])
    copy_prev.start()
    ghosts_xy(3, fb)
    inner_planes(fb, fa, outn_ref, 0, True)
    wait_ghost(0, 3)
    low_plane(3, fb, fa, outn_ref, 0, True)
    high_plane(3, fb, fa, outn_ref, 0, True)

    all_rows.wait_send()
    for k in range(STEPS):
        for kind in range(3):
            if kind or k != 1:
                wait_sent(kind, k)
    copy_prev.wait()


def put_out(p_ref, n_ref, p_hbm, n_hbm, sem):
    copies = [
        pltpu.make_async_copy(p_ref, p_hbm, sem.at[0]),
        pltpu.make_async_copy(n_ref, n_hbm, sem.at[1]),
    ]
    for c in copies:
        c.start()
    for c in copies:
        c.wait()


def body(traces, coupling, tap_shift, node_tile, node_cell, field_prev, field_now, speed_sq):
    vmem = pl.BlockSpec(memory_space=pltpu.VMEM)
    hbm = pl.BlockSpec(memory_space=pltpu.HBM)
    dma = pltpu.SemaphoreType.DMA
    n_dev = NT_AX * NGX * NGY
    last_two = pl.pallas_call(
        kernel,
        out_shape=(pltpu.VMEM((CZ, CX, CY), F32), pltpu.VMEM((CZ, CX, CY), F32)),
        in_specs=[hbm] + [vmem] * 5 + [hbm] * 3,
        out_specs=(vmem, vmem),
        scratch_shapes=[
            pltpu.VMEM((NT, COMP, NT), BF16),
            pltpu.VMEM((CZ, CX + 2 * PAD, CY), F32),
            pltpu.VMEM((CZ, CX + 2 * PAD, CY), F32),
            pltpu.VMEM((CZ, CX, CY), F32),
            pltpu.VMEM((CZ, CX, CY), F32),
            pltpu.VMEM((STEPS, 2, CX, CY), F32),
            pltpu.VMEM((STEPS, 2, CZ, CY), F32),
            pltpu.VMEM((STEPS, 2, CZ, CX), F32),
            pltpu.VMEM((STEPS, 2, CZ, CY), F32),
            pltpu.VMEM((STEPS, 2, CZ, CX), F32),
            pltpu.VMEM((CX, 128), F32),
            pltpu.VMEM((CZ * CX, CAP * 128), BF16),
            pltpu.VMEM((STEPS, CAP * 128, CY), BF16),
            pltpu.VMEM((STEPS, CAP * 128, CY), BF16),
            pltpu.VMEM((n_dev, 1, 128), F32),
            pltpu.VMEM((n_dev, 1, 128), F32),
            pltpu.VMEM((n_dev, 128), F32),
            dma((4,)),
            dma((1,)),
            dma((STEPS, 2)),
            dma((STEPS, 2)),
            dma((STEPS, 2)),
            dma((STEPS, 2)),
            dma((STEPS, 2)),
            dma((STEPS, 2)),
            dma((1,)),
            dma((1,)),
        ],
        compiler_params=pltpu.CompilerParams(
            collective_id=0, has_side_effects=True, vmem_limit_bytes=62_400_000
        ),
    )(
        traces,
        coupling.T,
        jnp.asarray(window_table()),
        tap_shift.reshape(1, -1),
        node_tile.reshape(1, -1),
        node_cell.reshape(1, -1),
        field_prev,
        field_now,
        speed_sq,
    )
    field = jax.ShapeDtypeStruct((CZ, CX, CY), F32)
    return pl.pallas_call(
        put_out,
        out_shape=(field, field),
        in_specs=[vmem] * 2,
        out_specs=(hbm, hbm),
        scratch_shapes=[dma((2,))],
        compiler_params=pltpu.CompilerParams(vmem_limit_bytes=1024 * 1024),
    )(*last_two)


def solution(mesh):
    everywhere = ("trace", "gx", "gy")
    placed = (
        P(everywhere, None, None),
        P(everywhere, None),
        P(everywhere),
        P(everywhere, None),
        P(everywhere),
        P("trace", "gx", "gy"),
        P("trace", "gx", "gy"),
        P("trace", "gx", "gy"),
    )
    return jax.shard_map(
        body,
        mesh=mesh,
        in_specs=placed,
        out_specs=(P("trace", "gx", "gy"), P("trace", "gx", "gy")),
        check_vma=False,
    )
```

```python
import math

import jax
import jax.numpy as jnp
import numpy as np
from jax import lax
from jax.experimental import pallas as pl
from jax.experimental.pallas import tpu as pltpu
from jax.sharding import PartitionSpec as P

NT = 256
STEPS = 4
RATE = 64
CZ, CX, CY = 8, 256, 256
NT_AX, NGX, NGY = 8, 4, 4
CAP = 4
COMP = 4
PAD = 8
ROWS = 32
MESH = pl.DeviceIdType.MESH
F32 = jnp.float32
BF16 = jnp.bfloat16


def window_table():
    u = (np.arange(NT)[None, :] + np.arange(NT)[:, None] - (NT - RATE // 2)).astype(np.float64)
    w = np.sinc(u / RATE) * 0.5 * (1.0 + np.cos(math.pi * u / (2.0 * RATE)))
    return np.where(np.abs(u) < 2.0 * RATE, w, 0.0).astype(np.float32)


def nt_dot(a, b, precision=None):
    return lax.dot_general(
        a, b, (((1,), (1,)), ((), ())), precision=precision, preferred_element_type=F32
    )


def kernel(
    traces_hbm, coup_ref, win_ref, shift_ref, tile_ref, cell_ref, prev_hbm, now_hbm, speed_hbm,
    outp_ref, outn_ref,
    tr, fa, fb, q, s_even, s_odd, gz, gi, gs, fo, so, gx_buf, gy_buf, px, py, hy, rows_1h, v_hi, v_lo, t1, b4, dense,
    lsem, osem, zs, zr, es, er, xs, xr, ys, yr, a_s, a_r,
):
    t = lax.axis_index("trace")
    gx = lax.axis_index("gx")
    gy = lax.axis_index("gy")
    n_dev = NT_AX * NGX * NGY
    me = (t * NGX + gx) * NGY + gy

    load_tr = pltpu.make_async_copy(traces_hbm, tr, lsem.at[3])
    load_tr.start()
    loads = [
        pltpu.make_async_copy(now_hbm, fa.at[:, pl.ds(PAD, CX), :], lsem.at[0]),
        pltpu.make_async_copy(prev_hbm, fb.at[:, pl.ds(PAD, CX), :], lsem.at[1]),
        pltpu.make_async_copy(speed_hbm, q, lsem.at[2]),
    ]
    for c in loads:
        c.start()

    def peer(d):
        k = lax.rem(me + d, n_dev)
        return k, (k // (NGX * NGY), lax.rem(k // NGY, NGX), lax.rem(k, NGY))

    barrier = pltpu.get_barrier_semaphore()

    def greet(d, carry):
        _, where = peer(d)
        pl.semaphore_signal(barrier, inc=1, device_id=where, device_id_type=MESH)
        return carry

    lax.fori_loop(1, n_dev, greet, 0)

    sides = (("trace", t, NT_AX), ("gx", gx, NGX), ("gy", gy, NGY))
    zsides = (sides[0],) * 3 + sides[1:]
    for buf, (_, pos, count) in zip((gz, gi, gs, gx_buf, gy_buf), zsides):
        for side in (0, 1):
            @pl.when(pos == (0 if side == 0 else count - 1))
            def _(buf=buf, side=side):
                for k in range(buf.shape[0]):
                    buf[k, side] = jnp.zeros(buf.shape[2:], buf.dtype)

    def halo(kind, k, d, src=None):
        axis, pos, count = sides[kind]
        ghost = (gz, gx_buf, gy_buf)[kind]
        ssem, rsem = ((zs, zr), (xs, xr), (ys, yr))[kind]
        if src is None:
            src = ghost.at[k, 1 - d]
        return pltpu.make_async_remote_copy(
            src_ref=src,
            dst_ref=ghost.at[k, 1 - d],
            send_sem=ssem.at[k, d],
            recv_sem=rsem.at[k, 1 - d],
            device_id={axis: jnp.clip(pos + 2 * d - 1, 0, count - 1)},
            device_id_type=MESH,
        )

    def faces(k, d):
        return [
            pltpu.make_async_remote_copy(
                src_ref=out.at[k - 1, d],
                dst_ref=ghost.at[k - 1, 1 - d],
                send_sem=ssem.at[k, d],
                recv_sem=rsem.at[k, 1 - d],
                device_id={"trace": jnp.clip(t + 2 * d - 1, 0, NT_AX - 1)},
                device_id_type=MESH,
            )
            for out, ghost, ssem, rsem in ((fo, gi, zs, zr), (so, gs, es, er))
        ]

    def face_exists(d):
        there = t + 2 * d - 1
        return jnp.logical_and(there >= 0, there < NT_AX)

    def send_face(k, d, f):
        v = f[d * (CZ - 1), pl.ds(PAD, CX), :].reshape(CX // 8, 8, CY)
        top = jnp.maximum(jnp.max(jnp.abs(v), axis=0), 1e-30)
        code = (v * (32767.0 / top)[None] + 32768.5).astype(jnp.int32) - 32768
        fo[k - 1, d] = code.reshape(CX, CY).astype(jnp.int16)
        so[k - 1, d] = top * (1.0 / 32767.0)

        @pl.when(face_exists(d))
        def _():
            for c in faces(k, d):
                c.start()

    def wait_face(k, side):
        @pl.when(face_exists(side))
        def _():
            for c in faces(k, 1 - side):
                c.wait_recv()

    def wait_faces_sent(k):
        for d in (0, 1):
            @pl.when(face_exists(d))
            def _(d=d):
                for c in faces(k, d):
                    c.wait_send()

    def exists(kind, d):
        _, pos, count = sides[kind]
        return pos > 0 if d == 0 else pos < count - 1

    def send(kind, k, d, src):
        @pl.when(exists(kind, d))
        def _():
            halo(kind, k, d, src).start()

    def wait_ghost(kind, k):
        for side in (0, 1):
            @pl.when(exists(kind, side))
            def _(side=side):
                halo(kind, k, 1 - side).wait_recv()

    def wait_sent(kind, k):
        for d in (0, 1):
            @pl.when(exists(kind, d))
            def _(d=d):
                halo(kind, k, d).wait_send()

    coup = jnp.transpose(
        jnp.concatenate([coup_ref[...].astype(F32), jnp.zeros((128 - COMP, NT), F32)], axis=0)
    )
    lane_i = lax.broadcasted_iota(jnp.int32, (NT, 128), 1)
    node_i = lax.broadcasted_iota(jnp.int32, (NT, 128), 0)
    comp = lane_i % COMP
    weight = coup[:, COMP - 1:COMP]
    for c in range(COMP - 2, -1, -1):
        weight = jnp.where(comp == c, coup[:, c:c + 1], weight)
    weight = jnp.where(lane_i // COMP == node_i % 32, weight, 0.0).astype(BF16)
    load_tr.wait()
    flat_tr = tr.reshape(NT * COMP, NT)
    combined = jnp.concatenate(
        [
            jnp.dot(
                weight[b * 32:(b + 1) * 32, :], flat_tr[b * 128:(b + 1) * 128, :],
                preferred_element_type=F32,
            )
            for b in range(NT // 32)
        ],
        axis=0,
    )

    at = nt_dot(win_ref[...], combined, lax.Precision.HIGHEST)
    shift = shift_ref[...]
    picked = lax.broadcasted_iota(jnp.int32, (RATE, NT), 0) == shift
    amps = [
        jnp.sum(jnp.where(picked, at[s * RATE:(s + 1) * RATE, :], 0.0), axis=0, keepdims=True)
        for s in range(STEPS)
    ]
    cell = cell_ref[...]
    cz = (cell // (CX * CY)).astype(F32)
    cx = ((cell // CY) % CX).astype(F32)
    cy = (cell % CY).astype(F32)
    hi = [a.astype(BF16).astype(F32) for a in amps]
    lo = [a - h for a, h in zip(amps, hi)]
    zero_row = jnp.zeros((1, NT), F32)
    vals = jnp.concatenate([cz, cx, cy] + hi + lo + [zero_row] * 5, axis=0).astype(BF16)
    onehot = lax.broadcasted_iota(jnp.int32, (n_dev, NT), 0) == tile_ref[...]
    onehot_f = jnp.where(onehot, 1.0, 0.0)
    before = jnp.where(
        lax.broadcasted_iota(jnp.int32, (NT, NT), 0) < lax.broadcasted_iota(jnp.int32, (NT, NT), 1),
        1.0, 0.0,
    ).astype(BF16)
    rank = jnp.dot(onehot_f.astype(BF16), before, preferred_element_type=F32)
    table = jnp.zeros((n_dev, 128), F32)
    for j in range(CAP):
        picks = jnp.where(rank == float(j), onehot_f, 0.0).astype(BF16)
        parts = []
        if j:
            parts.append(jnp.zeros((16 * j, NT), BF16))
        parts.append(vals)
        parts.append(jnp.zeros((128 - 16 * (j + 1), NT), BF16))
        table = table + nt_dot(picks, jnp.concatenate(parts, axis=0))
    t1[...] = table.reshape(n_dev, 1, 128)

    pl.semaphore_wait(barrier, n_dev - 1)

    def post(d, carry):
        k, where = peer(d)
        pltpu.make_async_remote_copy(
            src_ref=t1.at[k],
            dst_ref=b4.at[me],
            send_sem=a_s.at[0],
            recv_sem=a_r.at[0],
            device_id=where,
            device_id_type=MESH,
        ).start()
        return carry

    lax.fori_loop(1, n_dev, post, 0)
    b4[me] = t1[me]
    all_rows = pltpu.make_async_remote_copy(
        src_ref=t1.at[pl.ds(0, n_dev - 1)],
        dst_ref=b4.at[pl.ds(0, n_dev - 1)],
        send_sem=a_s.at[0],
        recv_sem=a_r.at[0],
        device_id=peer(1)[1],
        device_id_type=MESH,
    )

    send(0, 0, 0, now_hbm.at[0])
    send(0, 0, 1, now_hbm.at[CZ - 1])

    lane = lax.broadcasted_iota(jnp.int32, (CX, 128), 1)

    def pack_xy(k, f, beside_it=None):
        px[k, 0] = f[:, PAD, :]
        px[k, 1] = f[:, PAD + CX - 1, :]
        packed = jnp.zeros((CX, 128), F32)
        for z in range(CZ):
            left = pltpu.roll(f[z, pl.ds(PAD, CX), 0:128], z, 1) if z else f[z, pl.ds(PAD, CX), 0:128]
            packed = jnp.where(lane == z, left, packed)
            right = pltpu.roll(f[z, pl.ds(PAD, CX), 128:256], 9 + z, 1)
            packed = jnp.where(lane == 8 + z, right, packed)
        turned = jnp.transpose(packed)
        py[k, 0] = turned[0:8]
        py[k, 1] = turned[8:16]
        if beside_it is not None:
            beside_it()
        for d in (0, 1):
            send(1, k, d, px.at[k, d])
            send(2, k, d, py.at[k, d])

    for c in loads:
        c.wait()
    pack_xy(0, fa)

    def quarter(z, carry):
        q[z] = q[z] * 0.25
        return carry

    lax.fori_loop(0, CZ, quarter, 0)

    def scattered(s, r):
        total = jnp.dot(r, v_hi[s], preferred_element_type=F32) + jnp.dot(
            r, v_lo[s], preferred_element_type=F32
        )
        return total.reshape(2, CX, CY)

    sources = (s_even, s_odd)

    def source_ends(s):
        both = scattered(s, jnp.concatenate([rows_1h[0:CX], rows_1h[(CZ - 1) * CX:CZ * CX]], axis=0))
        sources[s % 2][0] = both[0]
        sources[s % 2][CZ - 1] = both[1]

    def source_pair(s, z):
        sources[s % 2][pl.ds(z, 2)] = scattered(
            s, rows_1h[pl.ds(pl.multiple_of(z * CX, CX), 2 * CX), :]
        )

    lane_r = lax.broadcasted_iota(jnp.int32, (ROWS, 128), 1)
    first, last = lane_r == 0, lane_r == 127

    def plane(cur, old, dst, dst_pad, z, below, above, source):
        for r0 in range(0, CX, ROWS):
            rows = pl.ds(PAD + r0, ROWS)
            flat = pl.ds(r0, ROWS)
            h = hy[flat, :]
            h_lo = pltpu.roll(h, lax.rem(128 - z, 128), 1)
            h_hi = pltpu.roll(h, 119 - z, 1)
            mid = []
            for half in (0, 1):
                cols = slice(128 * half, 128 * half + 128)
                mid.append(cur[z, rows, cols])
            fwd = [pltpu.roll(m, 1, 1) for m in mid]
            bwd = [pltpu.roll(m, 127, 1) for m in mid]
            ym = [jnp.where(first, h_lo, fwd[0]), jnp.where(first, fwd[0], fwd[1])]
            yp = [jnp.where(last, bwd[1], bwd[0]), jnp.where(last, h_hi, bwd[1])]
            for half in (0, 1):
                cols = slice(128 * half, 128 * half + 128)
                beside = below(rows, flat, cols) + above(rows, flat, cols)
                beside = beside + (
                    cur[z, pl.ds(PAD + r0 - 1, ROWS), cols] + cur[z, pl.ds(PAD + r0 + 1, ROWS), cols]
                )
                beside = beside + (ym[half] + yp[half])
                m = mid[half]
                beside = beside - 6.0 * m
                if source is not None:
                    beside = beside + source[z, flat, cols]
                dst[z, pl.ds(dst_pad + r0, ROWS), cols] = (
                    2.0 * m - old[z, rows, cols] + q[z, flat, cols] * beside
                )

    def ghosts_xy(k, cur):
        wait_ghost(1, k)
        wait_ghost(2, k)
        cur[:, PAD - 1, :] = gx_buf[k, 0]
        cur[:, PAD + CX, :] = gx_buf[k, 1]
        both = jnp.concatenate(
            [gy_buf[k, 0], gy_buf[k, 1], jnp.zeros((112, CX), F32)], axis=0
        )
        hy[...] = jnp.transpose(both)

    def inner_planes(cur, old, dst, dst_pad, source, ahead=None):
        def inner(i, carry):
            for z in (2 * i + 1, 2 * i + 2):
                plane(
                    cur, old, dst, dst_pad, z,
                    lambda rows, flat, cols: cur[z - 1, rows, cols],
                    lambda rows, flat, cols: cur[z + 1, rows, cols],
                    source,
                )
            if ahead is not None:
                source_pair(ahead, 2 * i + 1)
            return carry

        lax.fori_loop(0, CZ // 2 - 1, inner, 0)

    def end_plane(k, side, cur, old, dst, dst_pad, source):
        def ghost(rows, flat, cols):
            if k == 0:
                return gz[0, side, flat, cols]
            code = gi[k - 1, side, flat, cols].astype(jnp.int32).astype(F32)
            scale = gs[k - 1, side, :, cols]
            return (code.reshape(ROWS // 8, 8, 128) * scale[None]).reshape(ROWS, 128)

        plane(
            cur, old, dst, dst_pad, side * (CZ - 1),
            ghost,
            lambda rows, flat, cols: cur[1 + side * (CZ - 3), rows, cols],
            source,
        )

    ghosts_xy(0, fa)
    inner_planes(fa, fb, fb, PAD, None)
    wait_ghost(0, 0)
    end_plane(0, 0, fa, fb, fb, PAD, None)
    end_plane(0, 1, fa, fb, fb, PAD, None)

    all_rows.wait_recv()

    dense[...] = b4[...].reshape(n_dev, 128)
    nodes = dense[...]
    turned = jnp.transpose(nodes)
    row_of = []
    for j in range(CAP):
        zrow = turned[16 * j:16 * j + 1]
        xrow = turned[16 * j + 1:16 * j + 2]
        row_of.append((zrow * float(CX) + xrow).astype(jnp.int32))

    def fill_rows(z, carry):
        here = lax.broadcasted_iota(jnp.int32, (CX, 128), 0) + z * CX
        for j in range(CAP):
            rows_1h[pl.ds(pl.multiple_of(z * CX, CX), CX), j * 128:(j + 1) * 128] = jnp.where(
                here == row_of[j], 1.0, 0.0
            ).astype(BF16)
        return carry

    col_iota = lax.broadcasted_iota(jnp.int32, (n_dev, CY), 1)

    def fill_values(s_list):
        for j in range(CAP):
            at_col = col_iota == dense[:, 16 * j + 2:16 * j + 3].astype(jnp.int32)
            for s in s_list:
                for v, off in ((v_hi, 3), (v_lo, 7)):
                    c = 16 * j + off + s
                    v[s, j * 128:(j + 1) * 128, :] = jnp.where(
                        at_col, dense[:, c:c + 1], 0.0
                    ).astype(BF16)

    fill_rows(0, 0)
    fill_rows(CZ - 1, 0)
    fill_values((0,))
    source_ends(0)
    for side in (0, 1):
        z = side * (CZ - 1)
        fb[z, pl.ds(PAD, CX), :] = fb[z, pl.ds(PAD, CX), :] + q[z] * s_even[z]
        send_face(1, side, fb)
    lax.fori_loop(1, CZ - 1, fill_rows, 0)
    fill_values((1, 2, 3))

    def first_sources(i, carry):
        z = 2 * i + 1
        r = rows_1h[pl.ds(pl.multiple_of(z * CX, CX), 2 * CX), :]
        now = scattered(0, r)
        for n in (0, 1):
            fb[z + n, pl.ds(PAD, CX), :] = fb[z + n, pl.ds(PAD, CX), :] + q[z + n] * now[n]
        s_odd[pl.ds(z, 2)] = scattered(1, r)
        return carry

    lax.fori_loop(0, CZ // 2 - 1, first_sources, 0)
    pack_xy(1, fb, lambda: source_ends(1))

    off_chip = lax.rem(t, 2)
    for k in range(1, STEPS):
        cur = fb if k % 2 else fa
        nxt = fa if k % 2 else fb
        final = k == STEPS - 1
        dst, dst_pad = (outn_ref, 0) if final else (nxt, PAD)
        source = sources[k % 2]
        if final:
            copy_prev = pltpu.make_async_copy(cur.at[:, pl.ds(PAD, CX), :], outp_ref, osem.at[0])
            copy_prev.start()
        ghosts_xy(k, cur)
        inner_planes(cur, nxt, dst, dst_pad, source, None if final else k + 1)
        for side in (1 - off_chip, off_chip):
            wait_face(k, side)
            end_plane(k, side, cur, nxt, dst, dst_pad, source)
            if not final:
                send_face(k + 1, side, nxt)
        if not final:
            pack_xy(k + 1, nxt, lambda: source_ends(k + 1))

    all_rows.wait_send()
    wait_sent(0, 0)
    for k in range(STEPS):
        wait_sent(1, k)
        wait_sent(2, k)
        if k:
            wait_faces_sent(k)
    copy_prev.wait()


def put_out(p_ref, n_ref, p_hbm, n_hbm, sem):
    copies = [
        pltpu.make_async_copy(p_ref, p_hbm, sem.at[0]),
        pltpu.make_async_copy(n_ref, n_hbm, sem.at[1]),
    ]
    for c in copies:
        c.start()
    for c in copies:
        c.wait()


def body(traces, coupling, tap_shift, node_tile, node_cell, field_prev, field_now, speed_sq):
    vmem = pl.BlockSpec(memory_space=pltpu.VMEM)
    hbm = pl.BlockSpec(memory_space=pltpu.HBM)
    dma = pltpu.SemaphoreType.DMA
    n_dev = NT_AX * NGX * NGY
    last_two = pl.pallas_call(
        kernel,
        out_shape=(pltpu.VMEM((CZ, CX, CY), F32), pltpu.VMEM((CZ, CX, CY), F32)),
        in_specs=[hbm] + [vmem] * 5 + [hbm] * 3,
        out_specs=(vmem, vmem),
        scratch_shapes=[
            pltpu.VMEM((NT, COMP, NT), BF16),
            pltpu.VMEM((CZ, CX + 2 * PAD, CY), F32),
            pltpu.VMEM((CZ, CX + 2 * PAD, CY), F32),
            pltpu.VMEM((CZ, CX, CY), F32),
            pltpu.VMEM((CZ, CX, CY), F32),
            pltpu.VMEM((CZ, CX, CY), F32),
            pltpu.VMEM((1, 2, CX, CY), F32),
            pltpu.VMEM((STEPS - 1, 2, CX, CY), jnp.int16),
            pltpu.VMEM((STEPS - 1, 2, 8, CY), F32),
            pltpu.VMEM((STEPS - 1, 2, CX, CY), jnp.int16),
            pltpu.VMEM((STEPS - 1, 2, 8, CY), F32),
            pltpu.VMEM((STEPS, 2, CZ, CY), F32),
            pltpu.VMEM((STEPS, 2, CZ, CX), F32),
            pltpu.VMEM((STEPS, 2, CZ, CY), F32),
            pltpu.VMEM((STEPS, 2, CZ, CX), F32),
            pltpu.VMEM((CX, 128), F32),
            pltpu.VMEM((CZ * CX, CAP * 128), BF16),
            pltpu.VMEM((STEPS, CAP * 128, CY), BF16),
            pltpu.VMEM((STEPS, CAP * 128, CY), BF16),
            pltpu.VMEM((n_dev, 1, 128), F32),
            pltpu.VMEM((n_dev, 1, 128), F32),
            pltpu.VMEM((n_dev, 128), F32),
            dma((4,)),
            dma((1,)),
            dma((STEPS, 2)),
            dma((STEPS, 2)),
            dma((STEPS, 2)),
            dma((STEPS, 2)),
            dma((STEPS, 2)),
            dma((STEPS, 2)),
            dma((STEPS, 2)),
            dma((STEPS, 2)),
            dma((1,)),
            dma((1,)),
        ],
        compiler_params=pltpu.CompilerParams(
            collective_id=0, has_side_effects=True, vmem_limit_bytes=62_400_000
        ),
    )(
        traces,
        coupling.T,
        jnp.asarray(window_table()),
        tap_shift.reshape(1, -1),
        node_tile.reshape(1, -1),
        node_cell.reshape(1, -1),
        field_prev,
        field_now,
        speed_sq,
    )
    field = jax.ShapeDtypeStruct((CZ, CX, CY), F32)
    return pl.pallas_call(
        put_out,
        out_shape=(field, field),
        in_specs=[vmem] * 2,
        out_specs=(hbm, hbm),
        scratch_shapes=[dma((2,))],
        compiler_params=pltpu.CompilerParams(vmem_limit_bytes=1024 * 1024),
    )(*last_two)


def solution(mesh):
    everywhere = ("trace", "gx", "gy")
    placed = (
        P(everywhere, None, None),
        P(everywhere, None),
        P(everywhere),
        P(everywhere, None),
        P(everywhere),
        P("trace", "gx", "gy"),
        P("trace", "gx", "gy"),
        P("trace", "gx", "gy"),
    )
    return jax.shard_map(
        body,
        mesh=mesh,
        in_specs=placed,
        out_specs=(P("trace", "gx", "gy"), P("trace", "gx", "gy")),
        check_vma=False,
    )
```

```python
import math

import jax
import jax.numpy as jnp
import numpy as np
from jax import lax
from jax.experimental import pallas as pl
from jax.experimental.pallas import tpu as pltpu
from jax.sharding import PartitionSpec as P

NT = 256
STEPS = 4
RATE = 64
CZ, CX, CY = 8, 256, 256
NT_AX, NGX, NGY = 8, 4, 4
CAP = 4
COMP = 4
PAD = 8
ROWS = 32
MESH = pl.DeviceIdType.MESH
F32 = jnp.float32
BF16 = jnp.bfloat16


def window_table():
    u = (np.arange(NT)[None, :] + np.arange(NT)[:, None] - (NT - RATE // 2)).astype(np.float64)
    w = np.sinc(u / RATE) * 0.5 * (1.0 + np.cos(math.pi * u / (2.0 * RATE)))
    return np.where(np.abs(u) < 2.0 * RATE, w, 0.0).astype(np.float32)


def nt_dot(a, b, precision=None):
    return lax.dot_general(
        a, b, (((1,), (1,)), ((), ())), precision=precision, preferred_element_type=F32
    )


def kernel(
    traces_hbm, coup_ref, win_ref, shift_ref, tile_ref, cell_ref, prev_hbm, now_hbm, speed_hbm,
    outp_ref, outn_ref,
    tr, fa, fb, q, s_even, s_odd, gz, gi, gs, fo, so, gx_buf, gy_buf, px, py, hy, rows_1h, v_hi, v_lo, t1, b4, dense,
    lsem, osem, zs, zr, es, er, xs, xr, ys, yr, a_s, a_r,
):
    t = lax.axis_index("trace")
    gx = lax.axis_index("gx")
    gy = lax.axis_index("gy")
    n_dev = NT_AX * NGX * NGY
    me = (t * NGX + gx) * NGY + gy

    load_tr = pltpu.make_async_copy(traces_hbm, tr, lsem.at[3])
    load_tr.start()
    for f in (fa, fb):
        for row in (PAD - 1, PAD + CX):
            f[:, row:row + 1, :] = jnp.zeros((CZ, 1, CY), F32)
    loads = [
        pltpu.make_async_copy(now_hbm, fa.at[:, pl.ds(PAD, CX), :], lsem.at[0]),
        pltpu.make_async_copy(prev_hbm, fb.at[:, pl.ds(PAD, CX), :], lsem.at[1]),
        pltpu.make_async_copy(speed_hbm, q, lsem.at[2]),
    ]
    for c in loads:
        c.start()

    def peer(d):
        k = lax.rem(me + d, n_dev)
        return k, (k // (NGX * NGY), lax.rem(k // NGY, NGX), lax.rem(k, NGY))

    barrier = pltpu.get_barrier_semaphore()

    def greet(d, carry):
        _, where = peer(d)
        pl.semaphore_signal(barrier, inc=1, device_id=where, device_id_type=MESH)
        return carry

    lax.fori_loop(1, n_dev, greet, 0)

    sides = (("trace", t, NT_AX), ("gx", gx, NGX), ("gy", gy, NGY))
    zsides = (sides[0],) * 3 + sides[1:]
    for buf, (_, pos, count) in zip((gz, gi, gs, gx_buf, gy_buf), zsides):
        for side in (0, 1):
            @pl.when(pos == (0 if side == 0 else count - 1))
            def _(buf=buf, side=side):
                for k in range(buf.shape[0]):
                    buf[k, side] = jnp.zeros(buf.shape[2:], buf.dtype)

    def halo(kind, k, d, src=None):
        axis, pos, count = sides[kind]
        ghost = (gz, gx_buf, gy_buf)[kind]
        ssem, rsem = ((zs, zr), (xs, xr), (ys, yr))[kind]
        if src is None:
            src = ghost.at[k, 1 - d]
        return pltpu.make_async_remote_copy(
            src_ref=src,
            dst_ref=ghost.at[k, 1 - d],
            send_sem=ssem.at[k, d],
            recv_sem=rsem.at[k, 1 - d],
            device_id={axis: jnp.clip(pos + 2 * d - 1, 0, count - 1)},
            device_id_type=MESH,
        )

    def faces(k, d):
        return [
            pltpu.make_async_remote_copy(
                src_ref=out.at[k - 1, d],
                dst_ref=ghost.at[k - 1, 1 - d],
                send_sem=ssem.at[k, d],
                recv_sem=rsem.at[k, 1 - d],
                device_id={"trace": jnp.clip(t + 2 * d - 1, 0, NT_AX - 1)},
                device_id_type=MESH,
            )
            for out, ghost, ssem, rsem in ((fo, gi, zs, zr), (so, gs, es, er))
        ]

    def face_exists(d):
        there = t + 2 * d - 1
        return jnp.logical_and(there >= 0, there < NT_AX)

    def send_face(k, d, f):
        v = f[d * (CZ - 1), pl.ds(PAD, CX), :].reshape(CX // 8, 8, CY)
        top = jnp.maximum(jnp.max(jnp.abs(v), axis=0), 1e-30)
        code = (v * (32767.0 / top)[None] + 32768.5).astype(jnp.int32) - 32768
        fo[k - 1, d] = code.reshape(CX, CY).astype(jnp.int16)
        so[k - 1, d] = top * (1.0 / 32767.0)

        @pl.when(face_exists(d))
        def _():
            for c in faces(k, d):
                c.start()

    def wait_face(k, side):
        @pl.when(face_exists(side))
        def _():
            for c in faces(k, 1 - side):
                c.wait_recv()

    def wait_faces_sent(k):
        for d in (0, 1):
            @pl.when(face_exists(d))
            def _(d=d):
                for c in faces(k, d):
                    c.wait_send()

    def exists(kind, d):
        _, pos, count = sides[kind]
        return pos > 0 if d == 0 else pos < count - 1

    def send(kind, k, d, src):
        @pl.when(exists(kind, d))
        def _():
            halo(kind, k, d, src).start()

    def wait_ghost(kind, k):
        for side in (0, 1):
            @pl.when(exists(kind, side))
            def _(side=side):
                halo(kind, k, 1 - side).wait_recv()

    def wait_sent(kind, k):
        for d in (0, 1):
            @pl.when(exists(kind, d))
            def _(d=d):
                halo(kind, k, d).wait_send()

    coup = jnp.transpose(
        jnp.concatenate([coup_ref[...].astype(F32), jnp.zeros((128 - COMP, NT), F32)], axis=0)
    )
    lane_i = lax.broadcasted_iota(jnp.int32, (NT, 128), 1)
    node_i = lax.broadcasted_iota(jnp.int32, (NT, 128), 0)
    comp = lane_i % COMP
    weight = coup[:, COMP - 1:COMP]
    for c in range(COMP - 2, -1, -1):
        weight = jnp.where(comp == c, coup[:, c:c + 1], weight)
    weight = jnp.where(lane_i // COMP == node_i % 32, weight, 0.0).astype(BF16)
    load_tr.wait()
    flat_tr = tr.reshape(NT * COMP, NT)
    combined = jnp.concatenate(
        [
            jnp.dot(
                weight[b * 32:(b + 1) * 32, :], flat_tr[b * 128:(b + 1) * 128, :],
                preferred_element_type=F32,
            )
            for b in range(NT // 32)
        ],
        axis=0,
    )

    at = nt_dot(win_ref[...], combined, lax.Precision.HIGHEST)
    shift = shift_ref[...]
    picked = lax.broadcasted_iota(jnp.int32, (RATE, NT), 0) == shift
    amps = [
        jnp.sum(jnp.where(picked, at[s * RATE:(s + 1) * RATE, :], 0.0), axis=0, keepdims=True)
        for s in range(STEPS)
    ]
    cell = cell_ref[...]
    cz = (cell // (CX * CY)).astype(F32)
    cx = ((cell // CY) % CX).astype(F32)
    cy = (cell % CY).astype(F32)
    hi = [a.astype(BF16).astype(F32) for a in amps]
    lo = [a - h for a, h in zip(amps, hi)]
    zero_row = jnp.zeros((1, NT), F32)
    vals = jnp.concatenate([cz, cx, cy] + hi + lo + [zero_row] * 5, axis=0).astype(BF16)
    onehot = lax.broadcasted_iota(jnp.int32, (n_dev, NT), 0) == tile_ref[...]
    onehot_f = jnp.where(onehot, 1.0, 0.0)
    before = jnp.where(
        lax.broadcasted_iota(jnp.int32, (NT, NT), 0) < lax.broadcasted_iota(jnp.int32, (NT, NT), 1),
        1.0, 0.0,
    ).astype(BF16)
    rank = jnp.dot(onehot_f.astype(BF16), before, preferred_element_type=F32)
    table = jnp.zeros((n_dev, 128), F32)
    for j in range(CAP):
        picks = jnp.where(rank == float(j), onehot_f, 0.0).astype(BF16)
        parts = []
        if j:
            parts.append(jnp.zeros((16 * j, NT), BF16))
        parts.append(vals)
        parts.append(jnp.zeros((128 - 16 * (j + 1), NT), BF16))
        table = table + nt_dot(picks, jnp.concatenate(parts, axis=0))
    t1[...] = table.reshape(n_dev, 1, 128)

    pl.semaphore_wait(barrier, n_dev - 1)

    def post(d, carry):
        k, where = peer(d)
        pltpu.make_async_remote_copy(
            src_ref=t1.at[k],
            dst_ref=b4.at[me],
            send_sem=a_s.at[0],
            recv_sem=a_r.at[0],
            device_id=where,
            device_id_type=MESH,
        ).start()
        return carry

    lax.fori_loop(1, n_dev, post, 0)
    b4[me] = t1[me]
    all_rows = pltpu.make_async_remote_copy(
        src_ref=t1.at[pl.ds(0, n_dev - 1)],
        dst_ref=b4.at[pl.ds(0, n_dev - 1)],
        send_sem=a_s.at[0],
        recv_sem=a_r.at[0],
        device_id=peer(1)[1],
        device_id_type=MESH,
    )

    send(0, 0, 0, now_hbm.at[0])
    send(0, 0, 1, now_hbm.at[CZ - 1])

    lane = lax.broadcasted_iota(jnp.int32, (CX, 128), 1)

    parts_of = (tuple(range(1, CZ - 1)), (0, CZ - 1))

    def pack_xy(k, part, f, beside_it=None):
        n = 2 * k + part
        px[n, 0] = f[:, PAD, :]
        px[n, 1] = f[:, PAD + CX - 1, :]
        packed = jnp.zeros((CX, 128), F32)
        for z in parts_of[part]:
            left = pltpu.roll(f[z, pl.ds(PAD, CX), 0:128], z, 1) if z else f[z, pl.ds(PAD, CX), 0:128]
            packed = jnp.where(lane == z, left, packed)
            right = pltpu.roll(f[z, pl.ds(PAD, CX), 128:256], 9 + z, 1)
            packed = jnp.where(lane == 8 + z, right, packed)
        turned = jnp.transpose(packed)
        py[n, 0] = turned[0:8]
        py[n, 1] = turned[8:16]
        if beside_it is not None:
            beside_it()
        for d in (0, 1):
            send(1, n, d, px.at[n, d])
            send(2, n, d, py.at[n, d])

    for c in loads:
        c.wait()
    pack_xy(0, 0, fa)
    pack_xy(0, 1, fa)

    def quarter(z, carry):
        q[z] = q[z] * 0.25
        return carry

    lax.fori_loop(0, CZ, quarter, 0)

    def scattered(s, r):
        total = jnp.dot(r, v_hi[s], preferred_element_type=F32) + jnp.dot(
            r, v_lo[s], preferred_element_type=F32
        )
        return total.reshape(2, CX, CY)

    sources = (s_even, s_odd)

    def source_ends(s):
        both = scattered(s, jnp.concatenate([rows_1h[0:CX], rows_1h[(CZ - 1) * CX:CZ * CX]], axis=0))
        sources[s % 2][0] = both[0]
        sources[s % 2][CZ - 1] = both[1]

    def source_pair(s, z):
        sources[s % 2][pl.ds(z, 2)] = scattered(
            s, rows_1h[pl.ds(pl.multiple_of(z * CX, CX), 2 * CX), :]
        )

    lane_r = lax.broadcasted_iota(jnp.int32, (ROWS, 128), 1)
    first, last = lane_r == 0, lane_r == 127

    def plane(part, cur, old, dst, dst_pad, z, below, above, source):
        for r0 in range(0, CX, ROWS):
            rows = pl.ds(PAD + r0, ROWS)
            flat = pl.ds(r0, ROWS)
            if part:
                h = hy[part, flat, :]
                h_lo = pltpu.roll(h, lax.rem(128 - z, 128), 1)
                h_hi = pltpu.roll(h, 119 - z, 1)
            else:
                h_lo = h_hi = 0.0
            mid = []
            for half in (0, 1):
                cols = slice(128 * half, 128 * half + 128)
                mid.append(cur[z, rows, cols])
            fwd = [pltpu.roll(m, 1, 1) for m in mid]
            bwd = [pltpu.roll(m, 127, 1) for m in mid]
            ym = [jnp.where(first, h_lo, fwd[0]), jnp.where(first, fwd[0], fwd[1])]
            yp = [jnp.where(last, bwd[1], bwd[0]), jnp.where(last, h_hi, bwd[1])]
            for half in (0, 1):
                cols = slice(128 * half, 128 * half + 128)
                beside = below(rows, flat, cols) + above(rows, flat, cols)
                beside = beside + (
                    cur[z, pl.ds(PAD + r0 - 1, ROWS), cols] + cur[z, pl.ds(PAD + r0 + 1, ROWS), cols]
                )
                beside = beside + (ym[half] + yp[half])
                m = mid[half]
                beside = beside - 6.0 * m
                if source is not None:
                    beside = beside + source[z, flat, cols]
                dst[z, pl.ds(dst_pad + r0, ROWS), cols] = (
                    2.0 * m - old[z, rows, cols] + q[z, flat, cols] * beside
                )

    def ghosts_xy(k, part, cur):
        n = 2 * k + part
        wait_ghost(1, n)
        wait_ghost(2, n)
        if part:
            for z in parts_of[part]:
                cur[z, PAD - 1:PAD, :] = gx_buf[n, 0, z:z + 1]
                cur[z, PAD + CX:PAD + CX + 1, :] = gx_buf[n, 1, z:z + 1]
        both = jnp.concatenate(
            [gy_buf[n, 0], gy_buf[n, 1], jnp.zeros((112, CX), F32)], axis=0
        )
        hy[part] = jnp.transpose(both)

    def inner_planes(cur, old, dst, dst_pad, source, ahead=None):
        def inner(i, carry):
            for z in (2 * i + 1, 2 * i + 2):
                plane(
                    0, cur, old, dst, dst_pad, z,
                    lambda rows, flat, cols: cur[z - 1, rows, cols],
                    lambda rows, flat, cols: cur[z + 1, rows, cols],
                    source,
                )
            if ahead is not None:
                source_pair(ahead, 2 * i + 1)
            return carry

        lax.fori_loop(0, CZ // 2 - 1, inner, 0)

    def add_strips(k, cur, dst, dst_pad):
        ghosts_xy(k, 0, cur)

        def one(z, carry):
            for r0 in range(0, CX, ROWS):
                rows = pl.ds(dst_pad + r0, ROWS)
                flat = pl.ds(r0, ROWS)
                h = hy[0, flat, :]
                left = jnp.where(first, pltpu.roll(h, lax.rem(128 - z, 128), 1), 0.0)
                right = jnp.where(last, pltpu.roll(h, 119 - z, 1), 0.0)
                dst[z, rows, 0:128] = dst[z, rows, 0:128] + q[z, flat, 0:128] * left
                dst[z, rows, 128:256] = dst[z, rows, 128:256] + q[z, flat, 128:256] * right
            return carry

        lax.fori_loop(1, CZ - 1, one, 0)
        for z in range(1, CZ - 1):
            for side, row in ((0, 0), (1, CX - 1)):
                at_row = pl.ds(dst_pad + row, 1)
                dst[z, at_row, :] = (
                    dst[z, at_row, :] + q[z, row:row + 1, :] * gx_buf[2 * k, side, z:z + 1, :]
                )

    def end_plane(k, side, cur, old, dst, dst_pad, source):
        def ghost(rows, flat, cols):
            if k == 0:
                return gz[0, side, flat, cols]
            code = gi[k - 1, side, flat, cols].astype(jnp.int32).astype(F32)
            scale = gs[k - 1, side, :, cols]
            return (code.reshape(ROWS // 8, 8, 128) * scale[None]).reshape(ROWS, 128)

        plane(
            1, cur, old, dst, dst_pad, side * (CZ - 1),
            ghost,
            lambda rows, flat, cols: cur[1 + side * (CZ - 3), rows, cols],
            source,
        )

    inner_planes(fa, fb, fb, PAD, None)
    add_strips(0, fa, fb, PAD)
    ghosts_xy(0, 1, fa)
    wait_ghost(0, 0)
    end_plane(0, 0, fa, fb, fb, PAD, None)
    end_plane(0, 1, fa, fb, fb, PAD, None)

    all_rows.wait_recv()

    dense[...] = b4[...].reshape(n_dev, 128)
    nodes = dense[...]
    turned = jnp.transpose(nodes)
    row_of = []
    for j in range(CAP):
        zrow = turned[16 * j:16 * j + 1]
        xrow = turned[16 * j + 1:16 * j + 2]
        row_of.append((zrow * float(CX) + xrow).astype(jnp.int32))

    def fill_rows(z, carry):
        here = lax.broadcasted_iota(jnp.int32, (CX, 128), 0) + z * CX
        for j in range(CAP):
            rows_1h[pl.ds(pl.multiple_of(z * CX, CX), CX), j * 128:(j + 1) * 128] = jnp.where(
                here == row_of[j], 1.0, 0.0
            ).astype(BF16)
        return carry

    col_iota = lax.broadcasted_iota(jnp.int32, (n_dev, CY), 1)

    def fill_values(s_list):
        for j in range(CAP):
            at_col = col_iota == dense[:, 16 * j + 2:16 * j + 3].astype(jnp.int32)
            for s in s_list:
                for v, off in ((v_hi, 3), (v_lo, 7)):
                    c = 16 * j + off + s
                    v[s, j * 128:(j + 1) * 128, :] = jnp.where(
                        at_col, dense[:, c:c + 1], 0.0
                    ).astype(BF16)

    fill_rows(0, 0)
    fill_rows(CZ - 1, 0)
    fill_values((0,))
    source_ends(0)
    for side in (0, 1):
        z = side * (CZ - 1)
        fb[z, pl.ds(PAD, CX), :] = fb[z, pl.ds(PAD, CX), :] + q[z] * s_even[z]
        send_face(1, side, fb)
    lax.fori_loop(1, CZ - 1, fill_rows, 0)
    fill_values((1, 2, 3))

    def first_sources(i, carry):
        z = 2 * i + 1
        r = rows_1h[pl.ds(pl.multiple_of(z * CX, CX), 2 * CX), :]
        now = scattered(0, r)
        for n in (0, 1):
            fb[z + n, pl.ds(PAD, CX), :] = fb[z + n, pl.ds(PAD, CX), :] + q[z + n] * now[n]
        s_odd[pl.ds(z, 2)] = scattered(1, r)
        return carry

    lax.fori_loop(0, CZ // 2 - 1, first_sources, 0)
    pack_xy(1, 0, fb, lambda: source_ends(1))
    pack_xy(1, 1, fb)

    off_chip = lax.rem(t, 2)
    for k in range(1, STEPS):
        cur = fb if k % 2 else fa
        nxt = fa if k % 2 else fb
        final = k == STEPS - 1
        dst, dst_pad = (outn_ref, 0) if final else (nxt, PAD)
        source = sources[k % 2]
        if final:
            copy_prev = pltpu.make_async_copy(cur.at[:, pl.ds(PAD, CX), :], outp_ref, osem.at[0])
            copy_prev.start()
        inner_planes(cur, nxt, dst, dst_pad, source, None if final else k + 1)
        add_strips(k, cur, dst, dst_pad)
        if not final:
            pack_xy(k + 1, 0, nxt, lambda: source_ends(k + 1))
        ghosts_xy(k, 1, cur)
        for side in (1 - off_chip, off_chip):
            wait_face(k, side)
            end_plane(k, side, cur, nxt, dst, dst_pad, source)
            if not final:
                send_face(k + 1, side, nxt)
        if not final:
            pack_xy(k + 1, 1, nxt)

    all_rows.wait_send()
    wait_sent(0, 0)
    for k in range(STEPS):
        for n in (2 * k, 2 * k + 1):
            wait_sent(1, n)
            wait_sent(2, n)
        if k:
            wait_faces_sent(k)
    copy_prev.wait()


def put_out(p_ref, n_ref, p_hbm, n_hbm, sem):
    copies = [
        pltpu.make_async_copy(p_ref, p_hbm, sem.at[0]),
        pltpu.make_async_copy(n_ref, n_hbm, sem.at[1]),
    ]
    for c in copies:
        c.start()
    for c in copies:
        c.wait()


def body(traces, coupling, tap_shift, node_tile, node_cell, field_prev, field_now, speed_sq):
    vmem = pl.BlockSpec(memory_space=pltpu.VMEM)
    hbm = pl.BlockSpec(memory_space=pltpu.HBM)
    dma = pltpu.SemaphoreType.DMA
    n_dev = NT_AX * NGX * NGY
    last_two = pl.pallas_call(
        kernel,
        out_shape=(pltpu.VMEM((CZ, CX, CY), F32), pltpu.VMEM((CZ, CX, CY), F32)),
        in_specs=[hbm] + [vmem] * 5 + [hbm] * 3,
        out_specs=(vmem, vmem),
        scratch_shapes=[
            pltpu.VMEM((NT, COMP, NT), BF16),
            pltpu.VMEM((CZ, CX + 2 * PAD, CY), F32),
            pltpu.VMEM((CZ, CX + 2 * PAD, CY), F32),
            pltpu.VMEM((CZ, CX, CY), F32),
            pltpu.VMEM((CZ, CX, CY), F32),
            pltpu.VMEM((CZ, CX, CY), F32),
            pltpu.VMEM((1, 2, CX, CY), F32),
            pltpu.VMEM((STEPS - 1, 2, CX, CY), jnp.int16),
            pltpu.VMEM((STEPS - 1, 2, 8, CY), F32),
            pltpu.VMEM((STEPS - 1, 2, CX, CY), jnp.int16),
            pltpu.VMEM((STEPS - 1, 2, 8, CY), F32),
            pltpu.VMEM((2 * STEPS, 2, CZ, CY), F32),
            pltpu.VMEM((2 * STEPS, 2, CZ, CX), F32),
            pltpu.VMEM((2 * STEPS, 2, CZ, CY), F32),
            pltpu.VMEM((2 * STEPS, 2, CZ, CX), F32),
            pltpu.VMEM((2, CX, 128), F32),
            pltpu.VMEM((CZ * CX, CAP * 128), BF16),
            pltpu.VMEM((STEPS, CAP * 128, CY), BF16),
            pltpu.VMEM((STEPS, CAP * 128, CY), BF16),
            pltpu.VMEM((n_dev, 1, 128), F32),
            pltpu.VMEM((n_dev, 1, 128), F32),
            pltpu.VMEM((n_dev, 128), F32),
            dma((4,)),
            dma((1,)),
            dma((STEPS, 2)),
            dma((STEPS, 2)),
            dma((STEPS, 2)),
            dma((STEPS, 2)),
            dma((2 * STEPS, 2)),
            dma((2 * STEPS, 2)),
            dma((2 * STEPS, 2)),
            dma((2 * STEPS, 2)),
            dma((1,)),
            dma((1,)),
        ],
        compiler_params=pltpu.CompilerParams(
            collective_id=0, has_side_effects=True, vmem_limit_bytes=62_400_000
        ),
    )(
        traces,
        coupling.T,
        jnp.asarray(window_table()),
        tap_shift.reshape(1, -1),
        node_tile.reshape(1, -1),
        node_cell.reshape(1, -1),
        field_prev,
        field_now,
        speed_sq,
    )
    field = jax.ShapeDtypeStruct((CZ, CX, CY), F32)
    return pl.pallas_call(
        put_out,
        out_shape=(field, field),
        in_specs=[vmem] * 2,
        out_specs=(hbm, hbm),
        scratch_shapes=[dma((2,))],
        compiler_params=pltpu.CompilerParams(vmem_limit_bytes=1024 * 1024),
    )(*last_two)


def solution(mesh):
    everywhere = ("trace", "gx", "gy")
    placed = (
        P(everywhere, None, None),
        P(everywhere, None),
        P(everywhere),
        P(everywhere, None),
        P(everywhere),
        P("trace", "gx", "gy"),
        P("trace", "gx", "gy"),
        P("trace", "gx", "gy"),
    )
    return jax.shard_map(
        body,
        mesh=mesh,
        in_specs=placed,
        out_specs=(P("trace", "gx", "gy"), P("trace", "gx", "gy")),
        check_vma=False,
    )
```

```python
import math

import jax
import jax.numpy as jnp
import numpy as np
from jax import lax
from jax.experimental import pallas as pl
from jax.experimental.pallas import tpu as pltpu
from jax.sharding import PartitionSpec as P

NT = 256
STEPS = 4
RATE = 64
CZ, CX, CY = 8, 256, 256
NT_AX, NGX, NGY = 8, 4, 4
CAP = 4
COMP = 4
PAD = 8
ROWS = 32
MESH = pl.DeviceIdType.MESH
F32 = jnp.float32
BF16 = jnp.bfloat16


def window_table():
    u = (np.arange(NT)[None, :] + np.arange(NT)[:, None] - (NT - RATE // 2)).astype(np.float64)
    w = np.sinc(u / RATE) * 0.5 * (1.0 + np.cos(math.pi * u / (2.0 * RATE)))
    return np.where(np.abs(u) < 2.0 * RATE, w, 0.0).astype(np.float32)


def nt_dot(a, b, precision=None):
    return lax.dot_general(
        a, b, (((1,), (1,)), ((), ())), precision=precision, preferred_element_type=F32
    )


def kernel(
    traces_hbm, coup_ref, win_ref, shift_ref, tile_ref, cell_ref, prev_hbm, now_hbm, speed_hbm,
    outp_ref, outn_ref,
    tr, fa, fb, q, s_even, s_odd, gz, gi, gs, fo, so, gx_buf, gy_buf, px, py, hy, rows_1h, v_hi, v_lo, t1, b4, dense,
    lsem, osem, zs, zr, es, er, xs, xr, ys, yr, a_s, a_r,
):
    t = lax.axis_index("trace")
    gx = lax.axis_index("gx")
    gy = lax.axis_index("gy")
    n_dev = NT_AX * NGX * NGY
    me = (t * NGX + gx) * NGY + gy

    load_tr = pltpu.make_async_copy(traces_hbm, tr, lsem.at[3])
    load_tr.start()
    for f in (fa, fb):
        for row in (PAD - 1, PAD + CX):
            f[:, row:row + 1, :] = jnp.zeros((CZ, 1, CY), F32)
    loads = [
        pltpu.make_async_copy(now_hbm, fa.at[:, pl.ds(PAD, CX), :], lsem.at[0]),
        pltpu.make_async_copy(prev_hbm, fb.at[:, pl.ds(PAD, CX), :], lsem.at[1]),
        pltpu.make_async_copy(speed_hbm, q, lsem.at[2]),
    ]
    for c in loads:
        c.start()

    columns = [
        (lax.rem(gx + dx, NGX), lax.rem(gy + dy, NGY)) for dx in range(NGX) for dy in range(NGY)
    ]

    def to_all_others(act):
        for x, y in columns[1:]:
            act(t, x, y)

        def slab(d, carry):
            there = lax.rem(t + d, NT_AX)
            for x, y in columns:
                act(there, x, y)
            return carry

        lax.fori_loop(1, NT_AX, slab, 0)

    barrier = pltpu.get_barrier_semaphore()

    def greet(*where):
        pl.semaphore_signal(barrier, inc=1, device_id=where, device_id_type=MESH)

    to_all_others(greet)

    sides = (("trace", t, NT_AX), ("gx", gx, NGX), ("gy", gy, NGY))
    zsides = (sides[0],) * 3 + sides[1:]
    for buf, (_, pos, count) in zip((gz, gi, gs, gx_buf, gy_buf), zsides):
        for side in (0, 1):
            @pl.when(pos == (0 if side == 0 else count - 1))
            def _(buf=buf, side=side):
                for k in range(buf.shape[0]):
                    buf[k, side] = jnp.zeros(buf.shape[2:], buf.dtype)

    def halo(kind, k, d, src=None):
        axis, pos, count = sides[kind]
        ghost = (gz, gx_buf, gy_buf)[kind]
        ssem, rsem = ((zs, zr), (xs, xr), (ys, yr))[kind]
        if src is None:
            src = ghost.at[k, 1 - d]
        return pltpu.make_async_remote_copy(
            src_ref=src,
            dst_ref=ghost.at[k, 1 - d],
            send_sem=ssem.at[k, d],
            recv_sem=rsem.at[k, 1 - d],
            device_id={axis: jnp.clip(pos + 2 * d - 1, 0, count - 1)},
            device_id_type=MESH,
        )

    def faces(k, d):
        return [
            pltpu.make_async_remote_copy(
                src_ref=out.at[k - 1, d],
                dst_ref=ghost.at[k - 1, 1 - d],
                send_sem=ssem.at[k, d],
                recv_sem=rsem.at[k, 1 - d],
                device_id={"trace": jnp.clip(t + 2 * d - 1, 0, NT_AX - 1)},
                device_id_type=MESH,
            )
            for out, ghost, ssem, rsem in ((fo, gi, zs, zr), (so, gs, es, er))
        ]

    def face_exists(d):
        there = t + 2 * d - 1
        return jnp.logical_and(there >= 0, there < NT_AX)

    def send_face(k, d, f):
        v = f[d * (CZ - 1), pl.ds(PAD, CX), :].reshape(CX // 8, 8, CY)
        top = jnp.maximum(jnp.max(jnp.abs(v), axis=0), 1e-30)
        code = (v * (32767.0 / top)[None] + 32768.5).astype(jnp.int32) - 32768
        fo[k - 1, d] = code.reshape(CX, CY).astype(jnp.int16)
        so[k - 1, d] = top * (1.0 / 32767.0)

        @pl.when(face_exists(d))
        def _():
            for c in faces(k, d):
                c.start()

    def wait_face(k, side):
        @pl.when(face_exists(side))
        def _():
            for c in faces(k, 1 - side):
                c.wait_recv()

    def wait_faces_sent(k):
        for d in (0, 1):
            @pl.when(face_exists(d))
            def _(d=d):
                for c in faces(k, d):
                    c.wait_send()

    def exists(kind, d):
        _, pos, count = sides[kind]
        return pos > 0 if d == 0 else pos < count - 1

    def send(kind, k, d, src):
        @pl.when(exists(kind, d))
        def _():
            halo(kind, k, d, src).start()

    def wait_ghost(kind, k):
        for side in (0, 1):
            @pl.when(exists(kind, side))
            def _(side=side):
                halo(kind, k, 1 - side).wait_recv()

    def wait_sent(kind, k):
        for d in (0, 1):
            @pl.when(exists(kind, d))
            def _(d=d):
                halo(kind, k, d).wait_send()

    coup = jnp.transpose(
        jnp.concatenate([coup_ref[...].astype(F32), jnp.zeros((128 - COMP, NT), F32)], axis=0)
    )
    lane_i = lax.broadcasted_iota(jnp.int32, (NT, 128), 1)
    node_i = lax.broadcasted_iota(jnp.int32, (NT, 128), 0)
    comp = lane_i % COMP
    weight = coup[:, COMP - 1:COMP]
    for c in range(COMP - 2, -1, -1):
        weight = jnp.where(comp == c, coup[:, c:c + 1], weight)
    weight = jnp.where(lane_i // COMP == node_i % 32, weight, 0.0).astype(BF16)
    load_tr.wait()
    flat_tr = tr.reshape(NT * COMP, NT)
    combined = jnp.concatenate(
        [
            jnp.dot(
                weight[b * 32:(b + 1) * 32, :], flat_tr[b * 128:(b + 1) * 128, :],
                preferred_element_type=F32,
            )
            for b in range(NT // 32)
        ],
        axis=0,
    )

    at = nt_dot(win_ref[...], combined, lax.Precision.HIGHEST)
    shift = shift_ref[...]
    picked = lax.broadcasted_iota(jnp.int32, (RATE, NT), 0) == shift
    amps = [
        jnp.sum(jnp.where(picked, at[s * RATE:(s + 1) * RATE, :], 0.0), axis=0, keepdims=True)
        for s in range(STEPS)
    ]
    cell = cell_ref[...]
    cz = (cell // (CX * CY)).astype(F32)
    cx = ((cell // CY) % CX).astype(F32)
    cy = (cell % CY).astype(F32)
    hi = [a.astype(BF16).astype(F32) for a in amps]
    lo = [a - h for a, h in zip(amps, hi)]
    zero_row = jnp.zeros((1, NT), F32)
    vals = jnp.concatenate([cz, cx, cy] + hi + lo + [zero_row] * 5, axis=0).astype(BF16)
    onehot = lax.broadcasted_iota(jnp.int32, (n_dev, NT), 0) == tile_ref[...]
    onehot_f = jnp.where(onehot, 1.0, 0.0)
    before = jnp.where(
        lax.broadcasted_iota(jnp.int32, (NT, NT), 0) < lax.broadcasted_iota(jnp.int32, (NT, NT), 1),
        1.0, 0.0,
    ).astype(BF16)
    rank = jnp.dot(onehot_f.astype(BF16), before, preferred_element_type=F32)
    table = jnp.zeros((n_dev, 128), F32)
    for j in range(CAP):
        picks = jnp.where(rank == float(j), onehot_f, 0.0).astype(BF16)
        parts = []
        if j:
            parts.append(jnp.zeros((16 * j, NT), BF16))
        parts.append(vals)
        parts.append(jnp.zeros((128 - 16 * (j + 1), NT), BF16))
        table = table + nt_dot(picks, jnp.concatenate(parts, axis=0))
    t1[...] = table.reshape(n_dev, 1, 128)

    pl.semaphore_wait(barrier, n_dev - 1)

    def post(*where):
        pltpu.make_async_remote_copy(
            src_ref=t1.at[(where[0] * NGX + where[1]) * NGY + where[2]],
            dst_ref=b4.at[me],
            send_sem=a_s.at[0],
            recv_sem=a_r.at[0],
            device_id=where,
            device_id_type=MESH,
        ).start()

    to_all_others(post)
    b4[me] = t1[me]
    all_rows = pltpu.make_async_remote_copy(
        src_ref=t1.at[pl.ds(0, n_dev - 1)],
        dst_ref=b4.at[pl.ds(0, n_dev - 1)],
        send_sem=a_s.at[0],
        recv_sem=a_r.at[0],
        device_id=(t,) + columns[1],
        device_id_type=MESH,
    )

    send(0, 0, 0, now_hbm.at[0])
    send(0, 0, 1, now_hbm.at[CZ - 1])

    lane = lax.broadcasted_iota(jnp.int32, (CX, 128), 1)

    parts_of = (tuple(range(1, CZ - 1)), (0, CZ - 1))

    def pack_xy(k, part, f, beside_it=None):
        n = 2 * k + part
        px[n, 0] = f[:, PAD, :]
        px[n, 1] = f[:, PAD + CX - 1, :]
        packed = jnp.zeros((CX, 128), F32)
        for z in parts_of[part]:
            left = pltpu.roll(f[z, pl.ds(PAD, CX), 0:128], z, 1) if z else f[z, pl.ds(PAD, CX), 0:128]
            packed = jnp.where(lane == z, left, packed)
            right = pltpu.roll(f[z, pl.ds(PAD, CX), 128:256], 9 + z, 1)
            packed = jnp.where(lane == 8 + z, right, packed)
        turned = jnp.transpose(packed)
        py[n, 0] = turned[0:8]
        py[n, 1] = turned[8:16]
        if beside_it is not None:
            beside_it()
        for d in (0, 1):
            send(1, n, d, px.at[n, d])
            send(2, n, d, py.at[n, d])

    for c in loads:
        c.wait()
    pack_xy(0, 0, fa)
    pack_xy(0, 1, fa)

    def quarter(z, carry):
        q[z] = q[z] * 0.25
        return carry

    lax.fori_loop(0, CZ, quarter, 0)

    def scattered(s, r):
        total = jnp.dot(r, v_hi[s], preferred_element_type=F32) + jnp.dot(
            r, v_lo[s], preferred_element_type=F32
        )
        return total.reshape(2, CX, CY)

    sources = (s_even, s_odd)

    def source_ends(s):
        both = scattered(s, jnp.concatenate([rows_1h[0:CX], rows_1h[(CZ - 1) * CX:CZ * CX]], axis=0))
        sources[s % 2][0] = both[0]
        sources[s % 2][CZ - 1] = both[1]

    def source_pair(s, z):
        sources[s % 2][pl.ds(z, 2)] = scattered(
            s, rows_1h[pl.ds(pl.multiple_of(z * CX, CX), 2 * CX), :]
        )

    lane_r = lax.broadcasted_iota(jnp.int32, (ROWS, 128), 1)
    first, last = lane_r == 0, lane_r == 127

    def plane(part, cur, old, dst, dst_pad, z, below, above, source):
        for r0 in range(0, CX, ROWS):
            rows = pl.ds(PAD + r0, ROWS)
            flat = pl.ds(r0, ROWS)
            if part:
                h = hy[part, flat, :]
                h_lo = pltpu.roll(h, lax.rem(128 - z, 128), 1)
                h_hi = pltpu.roll(h, 119 - z, 1)
            else:
                h_lo = h_hi = 0.0
            mid = []
            for half in (0, 1):
                cols = slice(128 * half, 128 * half + 128)
                mid.append(cur[z, rows, cols])
            fwd = [pltpu.roll(m, 1, 1) for m in mid]
            bwd = [pltpu.roll(m, 127, 1) for m in mid]
            ym = [jnp.where(first, h_lo, fwd[0]), jnp.where(first, fwd[0], fwd[1])]
            yp = [jnp.where(last, bwd[1], bwd[0]), jnp.where(last, h_hi, bwd[1])]
            for half in (0, 1):
                cols = slice(128 * half, 128 * half + 128)
                beside = below(rows, flat, cols) + above(rows, flat, cols)
                beside = beside + (
                    cur[z, pl.ds(PAD + r0 - 1, ROWS), cols] + cur[z, pl.ds(PAD + r0 + 1, ROWS), cols]
                )
                beside = beside + (ym[half] + yp[half])
                m = mid[half]
                beside = beside - 6.0 * m
                if source is not None:
                    beside = beside + source[z, flat, cols]
                dst[z, pl.ds(dst_pad + r0, ROWS), cols] = (
                    2.0 * m - old[z, rows, cols] + q[z, flat, cols] * beside
                )

    def ghosts_xy(k, part, cur):
        n = 2 * k + part
        wait_ghost(1, n)
        wait_ghost(2, n)
        if part:
            for z in parts_of[part]:
                cur[z, PAD - 1:PAD, :] = gx_buf[n, 0, z:z + 1]
                cur[z, PAD + CX:PAD + CX + 1, :] = gx_buf[n, 1, z:z + 1]
        both = jnp.concatenate(
            [gy_buf[n, 0], gy_buf[n, 1], jnp.zeros((112, CX), F32)], axis=0
        )
        hy[part] = jnp.transpose(both)

    def inner_planes(cur, old, dst, dst_pad, source, ahead=None):
        def inner(i, carry):
            for z in (2 * i + 1, 2 * i + 2):
                plane(
                    0, cur, old, dst, dst_pad, z,
                    lambda rows, flat, cols: cur[z - 1, rows, cols],
                    lambda rows, flat, cols: cur[z + 1, rows, cols],
                    source,
                )
            if ahead is not None:
                source_pair(ahead, 2 * i + 1)
            return carry

        lax.fori_loop(0, CZ // 2 - 1, inner, 0)

    def add_strips(k, cur, dst, dst_pad):
        ghosts_xy(k, 0, cur)

        def one(z, carry):
            for r0 in range(0, CX, ROWS):
                rows = pl.ds(dst_pad + r0, ROWS)
                flat = pl.ds(r0, ROWS)
                h = hy[0, flat, :]
                left = jnp.where(first, pltpu.roll(h, lax.rem(128 - z, 128), 1), 0.0)
                right = jnp.where(last, pltpu.roll(h, 119 - z, 1), 0.0)
                dst[z, rows, 0:128] = dst[z, rows, 0:128] + q[z, flat, 0:128] * left
                dst[z, rows, 128:256] = dst[z, rows, 128:256] + q[z, flat, 128:256] * right
            return carry

        lax.fori_loop(1, CZ - 1, one, 0)
        for z in range(1, CZ - 1):
            for side, row in ((0, 0), (1, CX - 1)):
                at_row = pl.ds(dst_pad + row, 1)
                dst[z, at_row, :] = (
                    dst[z, at_row, :] + q[z, row:row + 1, :] * gx_buf[2 * k, side, z:z + 1, :]
                )

    def end_plane(k, side, cur, old, dst, dst_pad, source):
        def ghost(rows, flat, cols):
            if k == 0:
                return gz[0, side, flat, cols]
            code = gi[k - 1, side, flat, cols].astype(jnp.int32).astype(F32)
            scale = gs[k - 1, side, :, cols]
            return (code.reshape(ROWS // 8, 8, 128) * scale[None]).reshape(ROWS, 128)

        plane(
            1, cur, old, dst, dst_pad, side * (CZ - 1),
            ghost,
            lambda rows, flat, cols: cur[1 + side * (CZ - 3), rows, cols],
            source,
        )

    inner_planes(fa, fb, fb, PAD, None)
    add_strips(0, fa, fb, PAD)
    ghosts_xy(0, 1, fa)
    wait_ghost(0, 0)
    end_plane(0, 0, fa, fb, fb, PAD, None)
    end_plane(0, 1, fa, fb, fb, PAD, None)

    all_rows.wait_recv()

    dense[...] = b4[...].reshape(n_dev, 128)
    nodes = dense[...]
    turned = jnp.transpose(nodes)
    row_of = []
    for j in range(CAP):
        zrow = turned[16 * j:16 * j + 1]
        xrow = turned[16 * j + 1:16 * j + 2]
        row_of.append((zrow * float(CX) + xrow).astype(jnp.int32))

    def fill_rows(z, carry):
        here = lax.broadcasted_iota(jnp.int32, (CX, 128), 0) + z * CX
        for j in range(CAP):
            rows_1h[pl.ds(pl.multiple_of(z * CX, CX), CX), j * 128:(j + 1) * 128] = jnp.where(
                here == row_of[j], 1.0, 0.0
            ).astype(BF16)
        return carry

    col_iota = lax.broadcasted_iota(jnp.int32, (n_dev, CY), 1)

    def fill_values(s_list):
        for j in range(CAP):
            at_col = col_iota == dense[:, 16 * j + 2:16 * j + 3].astype(jnp.int32)
            for s in s_list:
                for v, off in ((v_hi, 3), (v_lo, 7)):
                    c = 16 * j + off + s
                    v[s, j * 128:(j + 1) * 128, :] = jnp.where(
                        at_col, dense[:, c:c + 1], 0.0
                    ).astype(BF16)

    fill_rows(0, 0)
    fill_rows(CZ - 1, 0)
    fill_values((0,))
    source_ends(0)
    for side in (0, 1):
        z = side * (CZ - 1)
        fb[z, pl.ds(PAD, CX), :] = fb[z, pl.ds(PAD, CX), :] + q[z] * s_even[z]
        send_face(1, side, fb)
    lax.fori_loop(1, CZ - 1, fill_rows, 0)
    fill_values((1, 2, 3))

    def first_sources(i, carry):
        z = 2 * i + 1
        r = rows_1h[pl.ds(pl.multiple_of(z * CX, CX), 2 * CX), :]
        now = scattered(0, r)
        for n in (0, 1):
            fb[z + n, pl.ds(PAD, CX), :] = fb[z + n, pl.ds(PAD, CX), :] + q[z + n] * now[n]
        s_odd[pl.ds(z, 2)] = scattered(1, r)
        return carry

    lax.fori_loop(0, CZ // 2 - 1, first_sources, 0)
    pack_xy(1, 0, fb, lambda: source_ends(1))
    pack_xy(1, 1, fb)

    off_chip = lax.rem(t, 2)
    for k in range(1, STEPS):
        cur = fb if k % 2 else fa
        nxt = fa if k % 2 else fb
        final = k == STEPS - 1
        dst, dst_pad = (outn_ref, 0) if final else (nxt, PAD)
        source = sources[k % 2]
        if final:
            copy_prev = pltpu.make_async_copy(cur.at[:, pl.ds(PAD, CX), :], outp_ref, osem.at[0])
            copy_prev.start()
        inner_planes(cur, nxt, dst, dst_pad, source, None if final else k + 1)
        add_strips(k, cur, dst, dst_pad)
        if not final:
            pack_xy(k + 1, 0, nxt, lambda: source_ends(k + 1))
        ghosts_xy(k, 1, cur)
        for side in (1 - off_chip, off_chip):
            wait_face(k, side)
            end_plane(k, side, cur, nxt, dst, dst_pad, source)
            if not final:
                send_face(k + 1, side, nxt)
        if not final:
            pack_xy(k + 1, 1, nxt)

    all_rows.wait_send()
    wait_sent(0, 0)
    for k in range(STEPS):
        for n in (2 * k, 2 * k + 1):
            wait_sent(1, n)
            wait_sent(2, n)
        if k:
            wait_faces_sent(k)
    copy_prev.wait()


def put_out(p_ref, n_ref, p_hbm, n_hbm, sem):
    copies = [
        pltpu.make_async_copy(p_ref, p_hbm, sem.at[0]),
        pltpu.make_async_copy(n_ref, n_hbm, sem.at[1]),
    ]
    for c in copies:
        c.start()
    for c in copies:
        c.wait()


def body(traces, coupling, tap_shift, node_tile, node_cell, field_prev, field_now, speed_sq):
    vmem = pl.BlockSpec(memory_space=pltpu.VMEM)
    hbm = pl.BlockSpec(memory_space=pltpu.HBM)
    dma = pltpu.SemaphoreType.DMA
    n_dev = NT_AX * NGX * NGY
    last_two = pl.pallas_call(
        kernel,
        out_shape=(pltpu.VMEM((CZ, CX, CY), F32), pltpu.VMEM((CZ, CX, CY), F32)),
        in_specs=[hbm] + [vmem] * 5 + [hbm] * 3,
        out_specs=(vmem, vmem),
        scratch_shapes=[
            pltpu.VMEM((NT, COMP, NT), BF16),
            pltpu.VMEM((CZ, CX + 2 * PAD, CY), F32),
            pltpu.VMEM((CZ, CX + 2 * PAD, CY), F32),
            pltpu.VMEM((CZ, CX, CY), F32),
            pltpu.VMEM((CZ, CX, CY), F32),
            pltpu.VMEM((CZ, CX, CY), F32),
            pltpu.VMEM((1, 2, CX, CY), F32),
            pltpu.VMEM((STEPS - 1, 2, CX, CY), jnp.int16),
            pltpu.VMEM((STEPS - 1, 2, 8, CY), F32),
            pltpu.VMEM((STEPS - 1, 2, CX, CY), jnp.int16),
            pltpu.VMEM((STEPS - 1, 2, 8, CY), F32),
            pltpu.VMEM((2 * STEPS, 2, CZ, CY), F32),
            pltpu.VMEM((2 * STEPS, 2, CZ, CX), F32),
            pltpu.VMEM((2 * STEPS, 2, CZ, CY), F32),
            pltpu.VMEM((2 * STEPS, 2, CZ, CX), F32),
            pltpu.VMEM((2, CX, 128), F32),
            pltpu.VMEM((CZ * CX, CAP * 128), BF16),
            pltpu.VMEM((STEPS, CAP * 128, CY), BF16),
            pltpu.VMEM((STEPS, CAP * 128, CY), BF16),
            pltpu.VMEM((n_dev, 1, 128), F32),
            pltpu.VMEM((n_dev, 1, 128), F32),
            pltpu.VMEM((n_dev, 128), F32),
            dma((4,)),
            dma((1,)),
            dma((STEPS, 2)),
            dma((STEPS, 2)),
            dma((STEPS, 2)),
            dma((STEPS, 2)),
            dma((2 * STEPS, 2)),
            dma((2 * STEPS, 2)),
            dma((2 * STEPS, 2)),
            dma((2 * STEPS, 2)),
            dma((1,)),
            dma((1,)),
        ],
        compiler_params=pltpu.CompilerParams(
            collective_id=0, has_side_effects=True, vmem_limit_bytes=62_400_000
        ),
    )(
        traces,
        coupling.T,
        jnp.asarray(window_table()),
        tap_shift.reshape(1, -1),
        node_tile.reshape(1, -1),
        node_cell.reshape(1, -1),
        field_prev,
        field_now,
        speed_sq,
    )
    field = jax.ShapeDtypeStruct((CZ, CX, CY), F32)
    return pl.pallas_call(
        put_out,
        out_shape=(field, field),
        in_specs=[vmem] * 2,
        out_specs=(hbm, hbm),
        scratch_shapes=[dma((2,))],
        compiler_params=pltpu.CompilerParams(vmem_limit_bytes=1024 * 1024),
    )(*last_two)


def solution(mesh):
    everywhere = ("trace", "gx", "gy")
    placed = (
        P(everywhere, None, None),
        P(everywhere, None),
        P(everywhere),
        P(everywhere, None),
        P(everywhere),
        P("trace", "gx", "gy"),
        P("trace", "gx", "gy"),
        P("trace", "gx", "gy"),
    )
    return jax.shard_map(
        body,
        mesh=mesh,
        in_specs=placed,
        out_specs=(P("trace", "gx", "gy"), P("trace", "gx", "gy")),
        check_vma=False,
    )
```

```python
import math

import jax
import jax.numpy as jnp
import numpy as np
from jax import lax
from jax.experimental import pallas as pl
from jax.experimental.pallas import tpu as pltpu
from jax.sharding import PartitionSpec as P

NT = 256
STEPS = 4
RATE = 64
CZ, CX, CY = 8, 256, 256
NT_AX, NGX, NGY = 8, 4, 4
CAP = 4
COMP = 4
PAD = 8
ROWS = 32
MESH = pl.DeviceIdType.MESH
F32 = jnp.float32
BF16 = jnp.bfloat16


def window_table():
    u = (np.arange(NT)[None, :] + np.arange(NT)[:, None] - (NT - RATE // 2)).astype(np.float64)
    w = np.sinc(u / RATE) * 0.5 * (1.0 + np.cos(math.pi * u / (2.0 * RATE)))
    return np.where(np.abs(u) < 2.0 * RATE, w, 0.0).astype(np.float32)


def nt_dot(a, b, precision=None):
    return lax.dot_general(
        a, b, (((1,), (1,)), ((), ())), precision=precision, preferred_element_type=F32
    )


def kernel(
    traces_hbm, coup_ref, win_ref, shift_ref, tile_ref, cell_ref, prev_hbm, now_hbm, speed_hbm,
    outp_ref, outn_ref,
    tr, fa, fb, q, s_even, s_odd, gz, gi, gs, fo, so, gx_buf, gy_buf, px, py, hy, rows_1h, v_hi, v_lo, t1, b4, dense,
    lsem, osem, zs, zr, es, er, xs, xr, ys, yr, a_s, a_r,
):
    t = lax.axis_index("trace")
    gx = lax.axis_index("gx")
    gy = lax.axis_index("gy")
    n_dev = NT_AX * NGX * NGY
    me = (t * NGX + gx) * NGY + gy

    load_tr = pltpu.make_async_copy(traces_hbm, tr, lsem.at[3])
    load_tr.start()
    for f in (fa, fb):
        for row in (PAD - 1, PAD + CX):
            f[:, row:row + 1, :] = jnp.zeros((CZ, 1, CY), F32)
    loads = [
        pltpu.make_async_copy(now_hbm, fa.at[:, pl.ds(PAD, CX), :], lsem.at[0]),
        pltpu.make_async_copy(prev_hbm, fb.at[:, pl.ds(PAD, CX), :], lsem.at[1]),
        pltpu.make_async_copy(speed_hbm, q, lsem.at[2]),
    ]
    for c in loads:
        c.start()

    columns = [
        (lax.rem(gx + dx, NGX), lax.rem(gy + dy, NGY)) for dx in range(NGX) for dy in range(NGY)
    ]

    def to_all_others(act):
        for x, y in columns[1:]:
            act(t, x, y)

        def slab(d, carry):
            there = lax.rem(t + d, NT_AX)
            for x, y in columns:
                act(there, x, y)
            return carry

        lax.fori_loop(1, NT_AX, slab, 0)

    barrier = pltpu.get_barrier_semaphore()

    def greet(*where):
        pl.semaphore_signal(barrier, inc=1, device_id=where, device_id_type=MESH)

    to_all_others(greet)

    sides = (("trace", t, NT_AX), ("gx", gx, NGX), ("gy", gy, NGY))
    zsides = (sides[0],) * 3 + sides[1:]
    for buf, (_, pos, count) in zip((gz, gi, gs, gx_buf, gy_buf), zsides):
        for side in (0, 1):
            @pl.when(pos == (0 if side == 0 else count - 1))
            def _(buf=buf, side=side):
                for k in range(buf.shape[0]):
                    buf[k, side] = jnp.zeros(buf.shape[2:], buf.dtype)

    def halo(kind, k, d, src=None):
        axis, pos, count = sides[kind]
        ghost = (gz, gx_buf, gy_buf)[kind]
        ssem, rsem = ((zs, zr), (xs, xr), (ys, yr))[kind]
        if src is None:
            src = ghost.at[k, 1 - d]
        return pltpu.make_async_remote_copy(
            src_ref=src,
            dst_ref=ghost.at[k, 1 - d],
            send_sem=ssem.at[k, d],
            recv_sem=rsem.at[k, 1 - d],
            device_id={axis: jnp.clip(pos + 2 * d - 1, 0, count - 1)},
            device_id_type=MESH,
        )

    def faces(k, d):
        return [
            pltpu.make_async_remote_copy(
                src_ref=out.at[k - 1, d],
                dst_ref=ghost.at[k - 1, 1 - d],
                send_sem=ssem.at[k, d],
                recv_sem=rsem.at[k, 1 - d],
                device_id={"trace": jnp.clip(t + 2 * d - 1, 0, NT_AX - 1)},
                device_id_type=MESH,
            )
            for out, ghost, ssem, rsem in ((fo, gi, zs, zr), (so, gs, es, er))
        ]

    def face_exists(d):
        there = t + 2 * d - 1
        return jnp.logical_and(there >= 0, there < NT_AX)

    def send_face(k, d, f):
        v = f[d * (CZ - 1), pl.ds(PAD, CX), :].reshape(CX // 8, 8, CY)
        top = jnp.maximum(jnp.max(jnp.abs(v), axis=0), 1e-30)
        code = (v * (32767.0 / top)[None] + 32768.5).astype(jnp.int32) - 32768
        fo[k - 1, d] = code.reshape(CX, CY).astype(jnp.int16)
        so[k - 1, d] = top * (1.0 / 32767.0)

        @pl.when(face_exists(d))
        def _():
            for c in faces(k, d):
                c.start()

    def wait_face(k, side):
        @pl.when(face_exists(side))
        def _():
            for c in faces(k, 1 - side):
                c.wait_recv()

    def wait_faces_sent(k):
        for d in (0, 1):
            @pl.when(face_exists(d))
            def _(d=d):
                for c in faces(k, d):
                    c.wait_send()

    def exists(kind, d):
        _, pos, count = sides[kind]
        return pos > 0 if d == 0 else pos < count - 1

    def send(kind, k, d, src):
        @pl.when(exists(kind, d))
        def _():
            halo(kind, k, d, src).start()

    def wait_ghost(kind, k):
        for side in (0, 1):
            @pl.when(exists(kind, side))
            def _(side=side):
                halo(kind, k, 1 - side).wait_recv()

    def wait_sent(kind, k):
        for d in (0, 1):
            @pl.when(exists(kind, d))
            def _(d=d):
                halo(kind, k, d).wait_send()

    coup = jnp.transpose(
        jnp.concatenate([coup_ref[...].astype(F32), jnp.zeros((128 - COMP, NT), F32)], axis=0)
    )
    lane_i = lax.broadcasted_iota(jnp.int32, (NT, 128), 1)
    node_i = lax.broadcasted_iota(jnp.int32, (NT, 128), 0)
    comp = lane_i % COMP
    weight = coup[:, COMP - 1:COMP]
    for c in range(COMP - 2, -1, -1):
        weight = jnp.where(comp == c, coup[:, c:c + 1], weight)
    weight = jnp.where(lane_i // COMP == node_i % 32, weight, 0.0).astype(BF16)
    load_tr.wait()
    flat_tr = tr.reshape(NT * COMP, NT)
    combined = jnp.concatenate(
        [
            jnp.dot(
                weight[b * 32:(b + 1) * 32, :], flat_tr[b * 128:(b + 1) * 128, :],
                preferred_element_type=F32,
            )
            for b in range(NT // 32)
        ],
        axis=0,
    )

    at = nt_dot(win_ref[...], combined, lax.Precision.HIGHEST)
    shift = shift_ref[...]
    picked = lax.broadcasted_iota(jnp.int32, (RATE, NT), 0) == shift
    amps = [
        jnp.sum(jnp.where(picked, at[s * RATE:(s + 1) * RATE, :], 0.0), axis=0, keepdims=True)
        for s in range(STEPS)
    ]
    cell = cell_ref[...]
    cz = (cell // (CX * CY)).astype(F32)
    cx = ((cell // CY) % CX).astype(F32)
    cy = (cell % CY).astype(F32)
    hi = [a.astype(BF16).astype(F32) for a in amps]
    lo = [a - h for a, h in zip(amps, hi)]
    zero_row = jnp.zeros((1, NT), F32)
    vals = jnp.concatenate([cz, cx, cy] + hi + lo + [zero_row] * 5, axis=0).astype(BF16)
    onehot = lax.broadcasted_iota(jnp.int32, (n_dev, NT), 0) == tile_ref[...]
    onehot_f = jnp.where(onehot, 1.0, 0.0)
    before = jnp.where(
        lax.broadcasted_iota(jnp.int32, (NT, NT), 0) < lax.broadcasted_iota(jnp.int32, (NT, NT), 1),
        1.0, 0.0,
    ).astype(BF16)
    rank = jnp.dot(onehot_f.astype(BF16), before, preferred_element_type=F32)
    table = jnp.zeros((n_dev, 128), F32)
    for j in range(CAP):
        picks = jnp.where(rank == float(j), onehot_f, 0.0).astype(BF16)
        parts = []
        if j:
            parts.append(jnp.zeros((16 * j, NT), BF16))
        parts.append(vals)
        parts.append(jnp.zeros((128 - 16 * (j + 1), NT), BF16))
        table = table + nt_dot(picks, jnp.concatenate(parts, axis=0))
    t1[...] = table.reshape(n_dev, 1, 128)

    pl.semaphore_wait(barrier, n_dev - 1)

    def post(*where):
        pltpu.make_async_remote_copy(
            src_ref=t1.at[(where[0] * NGX + where[1]) * NGY + where[2]],
            dst_ref=b4.at[me],
            send_sem=a_s.at[0],
            recv_sem=a_r.at[0],
            device_id=where,
            device_id_type=MESH,
        ).start()

    to_all_others(post)
    b4[me] = t1[me]
    all_rows = pltpu.make_async_remote_copy(
        src_ref=t1.at[pl.ds(0, n_dev - 1)],
        dst_ref=b4.at[pl.ds(0, n_dev - 1)],
        send_sem=a_s.at[0],
        recv_sem=a_r.at[0],
        device_id=(t,) + columns[1],
        device_id_type=MESH,
    )

    send(0, 0, 0, now_hbm.at[0])
    send(0, 0, 1, now_hbm.at[CZ - 1])

    lane = lax.broadcasted_iota(jnp.int32, (CX, 128), 1)

    parts_of = (tuple(range(1, CZ - 1)), (0, CZ - 1))

    def pack_xy(k, part, f, beside_it=None):
        n = 2 * k + part
        px[n, 0] = f[:, PAD, :]
        px[n, 1] = f[:, PAD + CX - 1, :]
        packed = jnp.zeros((CX, 128), F32)
        for z in parts_of[part]:
            left = pltpu.roll(f[z, pl.ds(PAD, CX), 0:128], z, 1) if z else f[z, pl.ds(PAD, CX), 0:128]
            packed = jnp.where(lane == z, left, packed)
            right = pltpu.roll(f[z, pl.ds(PAD, CX), 128:256], 9 + z, 1)
            packed = jnp.where(lane == 8 + z, right, packed)
        turned = jnp.transpose(packed)
        py[n, 0] = turned[0:8]
        py[n, 1] = turned[8:16]
        if beside_it is not None:
            beside_it()
        for d in (0, 1):
            send(1, n, d, px.at[n, d])
            send(2, n, d, py.at[n, d])

    for c in loads:
        c.wait()
    pack_xy(0, 0, fa)
    pack_xy(0, 1, fa)

    def quarter(z, carry):
        q[z] = q[z] * 0.25
        return carry

    lax.fori_loop(0, CZ, quarter, 0)

    def scattered(s, r):
        total = jnp.dot(r, v_hi[s], preferred_element_type=F32) + jnp.dot(
            r, v_lo[s], preferred_element_type=F32
        )
        return total.reshape(2, CX, CY)

    sources = (s_even, s_odd)

    def source_ends(s):
        both = scattered(s, jnp.concatenate([rows_1h[0:CX], rows_1h[(CZ - 1) * CX:CZ * CX]], axis=0))
        sources[s % 2][0] = both[0]
        sources[s % 2][CZ - 1] = both[1]

    def source_pair(s, z):
        sources[s % 2][pl.ds(z, 2)] = scattered(
            s, rows_1h[pl.ds(pl.multiple_of(z * CX, CX), 2 * CX), :]
        )

    lane_r = lax.broadcasted_iota(jnp.int32, (ROWS, 128), 1)
    first, last = lane_r == 0, lane_r == 127

    def plane(part, cur, old, dst, dst_pad, z, below, above, source):
        for r0 in range(0, CX, ROWS):
            rows = pl.ds(PAD + r0, ROWS)
            flat = pl.ds(r0, ROWS)
            if part:
                h = hy[part, flat, :]
                h_lo = pltpu.roll(h, (128 - z) % 128, 1)
                h_hi = pltpu.roll(h, 119 - z, 1)
            else:
                h_lo = h_hi = 0.0
            mid = []
            for half in (0, 1):
                cols = slice(128 * half, 128 * half + 128)
                mid.append(cur[z, rows, cols])
            fwd = [pltpu.roll(m, 1, 1) for m in mid]
            bwd = [pltpu.roll(m, 127, 1) for m in mid]
            ym = [jnp.where(first, h_lo, fwd[0]), jnp.where(first, fwd[0], fwd[1])]
            yp = [jnp.where(last, bwd[1], bwd[0]), jnp.where(last, h_hi, bwd[1])]
            for half in (0, 1):
                cols = slice(128 * half, 128 * half + 128)
                beside = below(rows, flat, cols) + above(rows, flat, cols)
                beside = beside + (
                    cur[z, pl.ds(PAD + r0 - 1, ROWS), cols] + cur[z, pl.ds(PAD + r0 + 1, ROWS), cols]
                )
                beside = beside + (ym[half] + yp[half])
                m = mid[half]
                beside = beside - 6.0 * m
                if source is not None:
                    beside = beside + source[z, flat, cols]
                dst[z, pl.ds(dst_pad + r0, ROWS), cols] = (
                    2.0 * m - old[z, rows, cols] + q[z, flat, cols] * beside
                )

    def ghosts_xy(k, part, cur):
        n = 2 * k + part
        wait_ghost(1, n)
        wait_ghost(2, n)
        if part:
            for z in parts_of[part]:
                cur[z, PAD - 1:PAD, :] = gx_buf[n, 0, z:z + 1]
                cur[z, PAD + CX:PAD + CX + 1, :] = gx_buf[n, 1, z:z + 1]
        both = jnp.concatenate(
            [gy_buf[n, 0], gy_buf[n, 1], jnp.zeros((112, CX), F32)], axis=0
        )
        hy[part] = jnp.transpose(both)

    def inner_planes(cur, old, dst, dst_pad, source, ahead=None):
        def inner(i, carry):
            for z in (2 * i + 1, 2 * i + 2):
                plane(
                    0, cur, old, dst, dst_pad, z,
                    lambda rows, flat, cols: cur[z - 1, rows, cols],
                    lambda rows, flat, cols: cur[z + 1, rows, cols],
                    source,
                )
            if ahead is not None:
                source_pair(ahead, 2 * i + 1)
            return carry

        lax.fori_loop(0, CZ // 2 - 1, inner, 0)

    def add_strips(k, cur, dst, dst_pad):
        ghosts_xy(k, 0, cur)

        def one(z, carry):
            for r0 in range(0, CX, ROWS):
                rows = pl.ds(dst_pad + r0, ROWS)
                flat = pl.ds(r0, ROWS)
                h = hy[0, flat, :]
                left = jnp.where(first, pltpu.roll(h, (128 - z) % 128, 1), 0.0)
                right = jnp.where(last, pltpu.roll(h, 119 - z, 1), 0.0)
                dst[z, rows, 0:128] = dst[z, rows, 0:128] + q[z, flat, 0:128] * left
                dst[z, rows, 128:256] = dst[z, rows, 128:256] + q[z, flat, 128:256] * right
            return carry

        for z in range(1, CZ - 1):
            one(z, 0)
        for z in range(1, CZ - 1):
            for side, row in ((0, 0), (1, CX - 1)):
                at_row = pl.ds(dst_pad + row, 1)
                dst[z, at_row, :] = (
                    dst[z, at_row, :] + q[z, row:row + 1, :] * gx_buf[2 * k, side, z:z + 1, :]
                )

    def end_plane(k, side, cur, old, dst, dst_pad, source):
        def ghost(rows, flat, cols):
            if k == 0:
                return gz[0, side, flat, cols]
            code = gi[k - 1, side, flat, cols].astype(jnp.int32).astype(F32)
            scale = gs[k - 1, side, :, cols]
            return (code.reshape(ROWS // 8, 8, 128) * scale[None]).reshape(ROWS, 128)

        plane(
            1, cur, old, dst, dst_pad, side * (CZ - 1),
            ghost,
            lambda rows, flat, cols: cur[1 + side * (CZ - 3), rows, cols],
            source,
        )

    inner_planes(fa, fb, fb, PAD, None)
    add_strips(0, fa, fb, PAD)
    ghosts_xy(0, 1, fa)
    wait_ghost(0, 0)
    end_plane(0, 0, fa, fb, fb, PAD, None)
    end_plane(0, 1, fa, fb, fb, PAD, None)

    all_rows.wait_recv()

    dense[...] = b4[...].reshape(n_dev, 128)
    nodes = dense[...]
    turned = jnp.transpose(nodes)
    row_of = []
    for j in range(CAP):
        zrow = turned[16 * j:16 * j + 1]
        xrow = turned[16 * j + 1:16 * j + 2]
        row_of.append((zrow * float(CX) + xrow).astype(jnp.int32))

    def fill_rows(z, carry):
        here = lax.broadcasted_iota(jnp.int32, (CX, 128), 0) + z * CX
        for j in range(CAP):
            rows_1h[pl.ds(pl.multiple_of(z * CX, CX), CX), j * 128:(j + 1) * 128] = jnp.where(
                here == row_of[j], 1.0, 0.0
            ).astype(BF16)
        return carry

    col_iota = lax.broadcasted_iota(jnp.int32, (n_dev, CY), 1)

    def fill_values(s_list):
        for j in range(CAP):
            at_col = col_iota == dense[:, 16 * j + 2:16 * j + 3].astype(jnp.int32)
            for s in s_list:
                for v, off in ((v_hi, 3), (v_lo, 7)):
                    c = 16 * j + off + s
                    v[s, j * 128:(j + 1) * 128, :] = jnp.where(
                        at_col, dense[:, c:c + 1], 0.0
                    ).astype(BF16)

    fill_rows(0, 0)
    fill_rows(CZ - 1, 0)
    fill_values((0,))
    source_ends(0)
    for side in (0, 1):
        z = side * (CZ - 1)
        fb[z, pl.ds(PAD, CX), :] = fb[z, pl.ds(PAD, CX), :] + q[z] * s_even[z]
        send_face(1, side, fb)
    lax.fori_loop(1, CZ - 1, fill_rows, 0)
    fill_values((1, 2, 3))

    def first_sources(i, carry):
        z = 2 * i + 1
        r = rows_1h[pl.ds(pl.multiple_of(z * CX, CX), 2 * CX), :]
        now = scattered(0, r)
        for n in (0, 1):
            fb[z + n, pl.ds(PAD, CX), :] = fb[z + n, pl.ds(PAD, CX), :] + q[z + n] * now[n]
        s_odd[pl.ds(z, 2)] = scattered(1, r)
        return carry

    for i in range(CZ // 2 - 1):
        first_sources(i, 0)
    pack_xy(1, 0, fb, lambda: source_ends(1))
    pack_xy(1, 1, fb)

    off_chip = lax.rem(t, 2)
    for k in range(1, STEPS):
        cur = fb if k % 2 else fa
        nxt = fa if k % 2 else fb
        final = k == STEPS - 1
        dst, dst_pad = (outn_ref, 0) if final else (nxt, PAD)
        source = sources[k % 2]
        if final:
            copy_prev = pltpu.make_async_copy(cur.at[:, pl.ds(PAD, CX), :], outp_ref, osem.at[0])
            copy_prev.start()
        inner_planes(cur, nxt, dst, dst_pad, source, None if final else k + 1)
        add_strips(k, cur, dst, dst_pad)
        if not final:
            pack_xy(k + 1, 0, nxt, lambda: source_ends(k + 1))
        ghosts_xy(k, 1, cur)
        for side in (1 - off_chip, off_chip):
            wait_face(k, side)
            end_plane(k, side, cur, nxt, dst, dst_pad, source)
            if not final:
                send_face(k + 1, side, nxt)
        if not final:
            pack_xy(k + 1, 1, nxt)

    all_rows.wait_send()
    wait_sent(0, 0)
    for k in range(STEPS):
        for n in (2 * k, 2 * k + 1):
            wait_sent(1, n)
            wait_sent(2, n)
        if k:
            wait_faces_sent(k)
    copy_prev.wait()


def put_out(p_ref, n_ref, p_hbm, n_hbm, sem):
    copies = [
        pltpu.make_async_copy(p_ref, p_hbm, sem.at[0]),
        pltpu.make_async_copy(n_ref, n_hbm, sem.at[1]),
    ]
    for c in copies:
        c.start()
    for c in copies:
        c.wait()


def body(traces, coupling, tap_shift, node_tile, node_cell, field_prev, field_now, speed_sq):
    vmem = pl.BlockSpec(memory_space=pltpu.VMEM)
    hbm = pl.BlockSpec(memory_space=pltpu.HBM)
    dma = pltpu.SemaphoreType.DMA
    n_dev = NT_AX * NGX * NGY
    last_two = pl.pallas_call(
        kernel,
        out_shape=(pltpu.VMEM((CZ, CX, CY), F32), pltpu.VMEM((CZ, CX, CY), F32)),
        in_specs=[hbm] + [vmem] * 5 + [hbm] * 3,
        out_specs=(vmem, vmem),
        scratch_shapes=[
            pltpu.VMEM((NT, COMP, NT), BF16),
            pltpu.VMEM((CZ, CX + 2 * PAD, CY), F32),
            pltpu.VMEM((CZ, CX + 2 * PAD, CY), F32),
            pltpu.VMEM((CZ, CX, CY), F32),
            pltpu.VMEM((CZ, CX, CY), F32),
            pltpu.VMEM((CZ, CX, CY), F32),
            pltpu.VMEM((1, 2, CX, CY), F32),
            pltpu.VMEM((STEPS - 1, 2, CX, CY), jnp.int16),
            pltpu.VMEM((STEPS - 1, 2, 8, CY), F32),
            pltpu.VMEM((STEPS - 1, 2, CX, CY), jnp.int16),
            pltpu.VMEM((STEPS - 1, 2, 8, CY), F32),
            pltpu.VMEM((2 * STEPS, 2, CZ, CY), F32),
            pltpu.VMEM((2 * STEPS, 2, CZ, CX), F32),
            pltpu.VMEM((2 * STEPS, 2, CZ, CY), F32),
            pltpu.VMEM((2 * STEPS, 2, CZ, CX), F32),
            pltpu.VMEM((2, CX, 128), F32),
            pltpu.VMEM((CZ * CX, CAP * 128), BF16),
            pltpu.VMEM((STEPS, CAP * 128, CY), BF16),
            pltpu.VMEM((STEPS, CAP * 128, CY), BF16),
            pltpu.VMEM((n_dev, 1, 128), F32),
            pltpu.VMEM((n_dev, 1, 128), F32),
            pltpu.VMEM((n_dev, 128), F32),
            dma((4,)),
            dma((1,)),
            dma((STEPS, 2)),
            dma((STEPS, 2)),
            dma((STEPS, 2)),
            dma((STEPS, 2)),
            dma((2 * STEPS, 2)),
            dma((2 * STEPS, 2)),
            dma((2 * STEPS, 2)),
            dma((2 * STEPS, 2)),
            dma((1,)),
            dma((1,)),
        ],
        compiler_params=pltpu.CompilerParams(
            collective_id=0, has_side_effects=True, vmem_limit_bytes=62_400_000
        ),
    )(
        traces,
        coupling.T,
        jnp.asarray(window_table()),
        tap_shift.reshape(1, -1),
        node_tile.reshape(1, -1),
        node_cell.reshape(1, -1),
        field_prev,
        field_now,
        speed_sq,
    )
    field = jax.ShapeDtypeStruct((CZ, CX, CY), F32)
    return pl.pallas_call(
        put_out,
        out_shape=(field, field),
        in_specs=[vmem] * 2,
        out_specs=(hbm, hbm),
        scratch_shapes=[dma((2,))],
        compiler_params=pltpu.CompilerParams(vmem_limit_bytes=1024 * 1024),
    )(*last_two)


def solution(mesh):
    everywhere = ("trace", "gx", "gy")
    placed = (
        P(everywhere, None, None),
        P(everywhere, None),
        P(everywhere),
        P(everywhere, None),
        P(everywhere),
        P("trace", "gx", "gy"),
        P("trace", "gx", "gy"),
        P("trace", "gx", "gy"),
    )
    return jax.shard_map(
        body,
        mesh=mesh,
        in_specs=placed,
        out_specs=(P("trace", "gx", "gy"), P("trace", "gx", "gy")),
        check_vma=False,
    )
```
